256 devices in a mesh: buf: 32 (over x, y, core), lat: 8 (over z).
Axes of the slice: x: 4, y: 4, z: 8, core: 2. Of those that a mesh axis runs over, the one named last changes fastest.
Arguments:
- buffer: bfloat16 [8192, 4096], P('buf'), may hold values from -6 to 6
- sample_rows: int32 [8192], P('lat'), may hold values from 0 to 8191, as said below
- window: bfloat16 [24576, 4096], P('buf'), may hold values from -6 to 6
- enc_scale: float32 [8192], P('lat'), may hold values from 0.5 to 2
- dec_bias: float32 [4096], replicated, may hold values from -3 to 3
Outputs:
- recon: bfloat16 [24576, 4096], P('buf', 'lat')
The draws below stay inside these ranges and needn't reach their ends.
Inputs may be any that keep to these rules, and one draw needn't show every extreme that they name: `sample_rows`: entry k names the buffer row sampled for reseeded latent k; shard s of the buffer holds rows s * 256 to (s + 1) * 256 - 1. In each aligned block of 32 entries at most 2 name rows of one shard, and in every block some shard gives exactly 2. In each owner's 1024 entries at most 64 name rows of one shard, and some shard gives exactly 64.
All inputs are finite; a program needn't handle non-finite values.
Results may differ from the reference program's by a relative error of at most 0.018.
Values may be sent and summed in bfloat16 or wider, within the bound.
A program may use at most 128 MiB of HBM per device.

```python
import math
import jax
import jax.numpy as jnp
from jax import lax

D = 4096
NEW_OWN = 1024
BUF_DEV = 256
NEW_LAT = 8192
WINDOW = 24576
BUF_ROWS = 8192
N_BUF = 32
N_LAT = 8


def draw_sample_rows(key, part):
    hot_key, order_key, slot_key, row_key = jax.random.split(key, 4)
    slot_count = NEW_OWN // N_BUF
    capacity = 2 + (slot_count - 1) // N_BUF
    hot_shard = jax.random.randint(hot_key, (N_LAT, 1, 1), 0, N_BUF)
    group_keys = jax.random.split(order_key, N_LAT * N_BUF)
    others = jax.vmap(lambda one_key: jax.random.permutation(one_key, N_BUF - 1))(group_keys)
    others = others.reshape(N_LAT, N_BUF, N_BUF - 1)
    slot_iota = jnp.arange(slot_count)
    extra = jnp.maximum(slot_iota - capacity, 0) % (N_BUF - 1)
    other_pick = jnp.take(others, extra, axis=2)
    other_pick = other_pick + (other_pick >= hot_shard).astype(other_pick.dtype)
    source = jnp.where(slot_iota[None, None, :] < capacity, hot_shard, other_pick)
    shuffle_keys = jax.random.split(slot_key, N_LAT * N_BUF)
    shuffle = jax.vmap(lambda one_key: jax.random.permutation(one_key, slot_count))(shuffle_keys)
    shuffle = shuffle.reshape(N_LAT, N_BUF, slot_count)
    source = jnp.take_along_axis(source, shuffle, axis=2)
    row_in_shard = jax.random.randint(row_key, (N_LAT, N_BUF, slot_count), 0, BUF_DEV)
    return (source * BUF_DEV + row_in_shard).reshape(-1).astype(jnp.int32)


def shard_levels(stream_key, shape, cuts, least, largest):
    gain, own = 1.0, jax.random.fold_in(stream_key, 6)
    for position, parts in cuts:
        draws = jnp.exp(jax.random.uniform(jax.random.fold_in(own, position), (parts,), jnp.float32, least / len(cuts), largest / len(cuts)))
        gain = gain * jnp.repeat(draws, shape[position] // parts).reshape([-1 if axis == position else 1 for axis in range(len(shape))])
    return gain


def normal_values(stream_key, dims, deviation, most, cuts=(), held_as=jnp.bfloat16):
    array = jax.random.normal(stream_key, dims, jnp.float32) * deviation
    if len(cuts) > 0:
        array = shard_levels(stream_key, dims, cuts, -0.22, 0.18) * array
    return jnp.clip(array, min=-most, max=most).astype(held_as)


def setup_inputs(seed: int = 0) -> dict:
    streams_of = jax.random.split(jax.random.key(seed), 6)
    return {
        "buffer": normal_values(streams_of[0], (BUF_ROWS, D), 1.0, 6.0, ((0, 32),)),
        "sample_rows": draw_sample_rows(jax.random.fold_in(streams_of[5], 71), 0),
        "window": normal_values(streams_of[2], (WINDOW, D), 1.0, 6.0, ((0, 32),)),
        "enc_scale": jnp.clip(jnp.exp(math.log(2.0) - 1.3862944 * jax.random.uniform(streams_of[3], (NEW_LAT,), jnp.float32) ** shard_levels(streams_of[3], (NEW_LAT,), ((0, 8),), -0.2, 0.2)), 0.5, 2.0),
        "dec_bias": normal_values(streams_of[4], (D,), 0.5, 3.0, (), jnp.float32),
    }


def reference(buffer, sample_rows, window, enc_scale, dec_bias):
    centered = (window.astype(jnp.float32) - dec_bias[None, :]).astype(jnp.bfloat16)
    index_blocks = sample_rows.reshape(N_LAT, NEW_OWN)
    scale_blocks = enc_scale.reshape(N_LAT, NEW_OWN)

    def owner_step(total, pieces):
        row_index, scale_block = pieces
        picked = jnp.take(buffer, row_index.astype(jnp.int32), axis=0).astype(jnp.float32)
        squares = lax.optimization_barrier(jnp.sum(picked * picked, axis=1, keepdims=True))
        inverse = lax.rsqrt(squares + 1e-06)
        units = (picked * inverse).astype(jnp.bfloat16)
        scores = lax.dot_general(centered, units, (((1,), (1,)), ((), ())), preferred_element_type=jnp.float32)
        active = jnp.maximum(scores * scale_block[None, :], 0.0).astype(jnp.bfloat16)
        partial_value = jnp.dot(active, units, preferred_element_type=jnp.float32).astype(jnp.bfloat16)
        return (total + partial_value.astype(jnp.float32), None)
    start = jnp.zeros((window.shape[0], window.shape[1]), jnp.float32)
    total, unused = lax.scan(owner_step, start, (index_blocks, scale_blocks))
    return (total + dec_bias[None, :]).astype(jnp.bfloat16)
```

```python
import jax
import jax.numpy as jnp
from jax import lax
from jax.experimental import pallas as pl
from jax.experimental.pallas import tpu as pltpu
from jax.sharding import PartitionSpec as P

MESH = pl.DeviceIdType.MESH
NT = (((1,), (1,)), ((), ()))


def rem(value, size):
    return lax.rem(value, size)


def fused(
    rows_ref, buf_ref, win_hbm, scale_ref, bias_ref, out_ref,
    stage, send, recv, picked, units, cen, act, part, flow_r, flow_l,
    win_sem, own_sem, a2a_send, a2a_recv, ag_send, ag_recv, ag_recv2, rs_send, rs_recv,
):
    me = lax.axis_index("buf")
    owner = lax.axis_index("lat")
    core = rem(me, 2)
    chip = me // 2
    x, y = chip // 4, rem(chip, 4)
    a = x + core * (y - x)
    b = y + core * (x - y)
    right, left = rem(owner + 1, 8), rem(owner + 7, 8)

    barrier = pltpu.get_barrier_semaphore()

    def greet(k, carry):
        pl.semaphore_signal(
            barrier, inc=1, device_id={"buf": rem(me + k, 32)}, device_id_type=MESH
        )
        return carry

    lax.fori_loop(1, 32, greet, 0)
    for near in (right, left):
        pl.semaphore_signal(barrier, inc=1, device_id={"lat": near}, device_id_type=MESH)

    win_copy = pltpu.make_async_copy(win_hbm, cen, win_sem)
    win_copy.start()

    rows = rows_ref[...]
    offset = rows - me * 256
    mine = (offset >= 0) & (offset < 256)
    key = (lax.broadcasted_iota(jnp.int32, (32, 32), 1) * 256 + offset).astype(jnp.float32)
    first = jnp.min(jnp.where(mine, key, 8191.0), axis=1, keepdims=True).astype(jnp.int32)
    last = jnp.max(jnp.where(mine, key, 0.0), axis=1, keepdims=True).astype(jnp.int32)
    lane = lax.broadcasted_iota(jnp.int32, (32, 256), 1)
    for r, chosen in enumerate((first, last)):
        hot = (jnp.bitwise_and(chosen, 255) == lane).astype(jnp.float32).astype(jnp.bfloat16)
        for q in range(8):
            piece = jnp.dot(
                hot, buf_ref[:, q * 512:(q + 1) * 512], preferred_element_type=jnp.float32
            )
            for g in range(4):
                stage[g, pl.ds(r * 8 + q, 32, stride=16), :] = piece[:, g * 128:(g + 1) * 128]
    for g in range(4):
        send[:, g * 128:(g + 1) * 128] = stage[g].astype(jnp.bfloat16)

    pl.semaphore_wait(barrier, 33)

    def block_of(device):
        dc = rem(device, 2)
        dchip = device // 2
        dx, dy = dchip // 4, rem(dchip, 4)
        return dc * 16 + (dy + dc * (dx - dy)) * 4 + dx + dc * (dy - dx)

    def tile16(ref, index):
        return ref.at[pl.ds(pl.multiple_of(index * 16, 16), 16), :]

    def push(k, carry):
        target = rem(me + k, 32)
        pltpu.make_async_remote_copy(
            src_ref=tile16(send, block_of(target)),
            dst_ref=tile16(recv, me),
            send_sem=a2a_send,
            recv_sem=a2a_recv,
            device_id={"buf": target},
            device_id_type=MESH,
        ).start()
        return carry

    lax.fori_loop(1, 32, push, 0)
    my_block = core * 16 + b * 4 + a
    own_copy = pltpu.make_async_copy(tile16(send, my_block), tile16(recv, me), own_sem)
    own_copy.start()

    win_copy.wait()

    def center(t, carry):
        at = pl.ds(pl.multiple_of(t * 32, 32), 32)
        cen[at, :] = (cen[at, :].astype(jnp.float32) - bias_ref[...]).astype(jnp.bfloat16)
        return carry

    lax.fori_loop(0, 24, center, 0)

    own_copy.wait()
    pltpu.make_async_copy(recv.at[pl.ds(0, 496), :], recv.at[pl.ds(0, 496), :], a2a_recv).wait()

    own = jnp.broadcast_to(rows_ref[pl.ds(my_block, 1), :], (32, 32))
    own = lax.shift_right_logical(own, 8).astype(jnp.float32)
    entry = lax.broadcasted_iota(jnp.int32, (32, 32), 0)
    peer = lax.broadcasted_iota(jnp.int32, (32, 32), 1)
    source = jnp.sum(jnp.where(entry == peer, own, 0.0), axis=1, keepdims=True)
    twin = (own == source) & (peer < entry)
    rank = jnp.sum(jnp.where(twin, 1.0, 0.0), axis=1, keepdims=True)
    code = (source * 16.0 + rank * 8.0).astype(jnp.int32)
    code = jnp.concatenate([code + q for q in range(8)], axis=0)
    hot = code == lax.broadcasted_iota(jnp.int32, (256, 512), 1)
    hot = hot.astype(jnp.float32).astype(jnp.bfloat16)
    picked[...] = jnp.dot(hot, recv[...], preferred_element_type=jnp.float32)
    squares = jnp.zeros((32, 512), jnp.float32)
    for q in range(8):
        value = picked[q * 32:q * 32 + 32, :]
        squares += value * value
    inverse = lax.rsqrt(jnp.sum(squares, axis=1, keepdims=True) + 1e-06)
    mine_at = pl.ds(pl.multiple_of(my_block * 32, 32), 32)
    for q in range(8):
        value = picked[q * 32:q * 32 + 32, :]
        units[mine_at, q * 512:q * 512 + 512] = (value * inverse).astype(jnp.bfloat16)

    def block_at(da, db):
        return core * 16 + rem(b + db + 4, 4) * 4 + rem(a + da + 4, 4)

    def device_at(da, db):
        pa, pb = rem(a + da + 4, 4), rem(b + db + 4, 4)
        px, py = pa + core * (pb - pa), pb + core * (pa - pb)
        return (px * 4 + py) * 2 + core

    sibling = me + 1 - 2 * core
    sent = []

    def block_copy(block, target, count=32, half=0):
        at = units.at[pl.ds(pl.multiple_of(block * 32 + half * 16, 16), count), :]
        sem = ag_recv2 if half else ag_recv
        return pltpu.make_async_remote_copy(
            src_ref=at, dst_ref=at, send_sem=ag_send.at[len(sent)], recv_sem=sem.at[block],
            device_id={"buf": target}, device_id_type=MESH,
        )

    def give(block, target, count=32, half=0):
        copy = block_copy(block, target, count, half)
        copy.start()
        sent.append(copy)

    def arrive(block, count=32, half=0):
        at = units.at[pl.ds(pl.multiple_of(block * 32 + half * 16, 16), count), :]
        sem = ag_recv2 if half else ag_recv
        pltpu.make_async_copy(at, at, sem.at[block]).wait()

    def spread(block):
        give(block, device_at(0, 1))
        give(block, device_at(0, -1))
        give(block, sibling)

    give(my_block, device_at(1, 0))
    give(my_block, device_at(-1, 0))
    spread(my_block)

    block = block_at(-1, 0)
    arrive(block)
    give(block, device_at(1, 0), 16, 0)
    spread(block)
    block = block_at(1, 0)
    arrive(block)
    give(block, device_at(-1, 0), 16, 1)
    spread(block)

    def second(da):
        block = block_at(da, -1)
        arrive(block)
        give(block, device_at(0, 1), 16, 0)
        give(block, sibling)
        block = block_at(da, 1)
        arrive(block)
        give(block, device_at(0, -1), 16, 1)
        give(block, sibling)

    second(0)
    block = block_at(2, 0)
    arrive(block, 16, 0)
    arrive(block, 16, 1)
    spread(block)
    second(-1)
    second(1)
    second(2)

    def encode(group):
        at = pl.ds(pl.multiple_of(group * 256, 256), 256)
        scores = lax.dot_general(
            cen[...], units[at, :], NT, preferred_element_type=jnp.float32
        )
        act[:, at] = jnp.maximum(scores * scale_ref[:, at], 0.0).astype(jnp.bfloat16)

    other = 1 - core
    other_b = x + core * (y - x)
    mine_near = core * 2 + b // 2
    mine_far = core * 2 + 1 - b // 2
    other_near = other * 2 + other_b // 2
    other_far = other * 2 + 1 - other_b // 2

    def arrive_group(group):
        def one(i, carry):
            arrive(group * 8 + i)
            return carry

        lax.fori_loop(0, 8, one, 0)

    encode(mine_near)
    for da in (0, -1, 1, 2):
        block = block_at(da, 2)
        arrive(block, 16, 0)
        arrive(block, 16, 1)
        give(block, sibling)
    arrive_group(other_near)
    encode(other_near)
    encode(mine_far)
    arrive_group(other_far)
    encode(other_far)

    def decode(target):
        columns = pl.ds(pl.multiple_of(target * 512, 512), 512)
        value = jnp.dot(act[...], units[:, columns], preferred_element_type=jnp.float32)
        part[target] = value.astype(jnp.bfloat16)

    def half_of(ref, half):
        return ref.at[pl.ds(pl.multiple_of(half * 384, 384), 384), :]

    def rs_copy(i, source, flow, way):
        return pltpu.make_async_remote_copy(
            src_ref=source, dst_ref=flow.at[i],
            send_sem=rs_send.at[way, i], recv_sem=rs_recv.at[way, i],
            device_id={"lat": left if way else right}, device_id_type=MESH,
        )

    def rs_wait(i, flow, way):
        pltpu.make_async_copy(flow.at[i], flow.at[i], rs_recv.at[way, i]).wait()

    across = rem(owner + 4, 8)
    decode(across)
    rs_copy(0, half_of(part.at[across], 0), flow_r, 0).start()
    rs_copy(0, half_of(part.at[across], 1), flow_l, 1).start()

    def decode_pair(i, carry):
        decode(rem(owner + 3 + 2 * i, 8))
        return carry

    lax.fori_loop(0, 2, decode_pair, 0)
    rs_copy(1, half_of(part.at[rem(owner + 3, 8)], 1), flow_r, 0).start()
    rs_copy(1, half_of(part.at[rem(owner + 5, 8)], 0), flow_l, 1).start()

    def decode_rest(i, carry):
        decode(rem(owner + 6 + i, 8))
        return carry

    lax.fori_loop(0, 5, decode_rest, 0)

    def hop(i, carry):
        step = (i + 1) // 2
        for way, flow in ((0, flow_r), (1, flow_l)):
            half = rem(i + way, 2)
            target = rem(owner + 4 - step, 8) if way == 0 else rem(owner + 4 + step, 8)
            rs_wait(i - 2, flow, way)
            at = pl.ds(pl.multiple_of(half * 384, 384), 384)
            total = flow[i - 2].astype(jnp.float32) + part[target, at, :].astype(jnp.float32)
            flow[i - 2] = total.astype(jnp.bfloat16)
            rs_copy(i, flow.at[i - 2], flow, way).start()
        return carry

    lax.fori_loop(2, 7, hop, 0)

    bias = bias_ref[:, pl.ds(pl.multiple_of(owner * 512, 512), 512)]
    for i, j, half in ((5, 5, None), (6, 6, None)):
        rs_wait(i, flow_r, 0)
        rs_wait(j, flow_l, 1)
    for half in range(2):
        rows_at = slice(half * 384, half * 384 + 384)
        total = part[owner, rows_at, :].astype(jnp.float32) + bias
        total += flow_r[6 - half].astype(jnp.float32) + flow_l[5 + half].astype(jnp.float32)
        out_ref[rows_at, :] = total.astype(jnp.bfloat16)

    pltpu.make_async_copy(send.at[pl.ds(0, 496), :], send.at[pl.ds(0, 496), :], a2a_send).wait()
    for copy in sent:
        copy.wait_send()

    def drain(i, carry):
        for way in range(2):
            pltpu.make_async_copy(flow_r.at[i], flow_r.at[i], rs_send.at[way, i]).wait()
        return carry

    lax.fori_loop(0, 7, drain, 0)


def on_device(buffer, sample_rows, window, enc_scale, dec_bias):
    vmem = pl.BlockSpec(memory_space=pltpu.VMEM)
    call = pl.pallas_call(
        fused,
        out_shape=jax.ShapeDtypeStruct((768, 512), jnp.bfloat16),
        in_specs=[
            vmem, vmem, pl.BlockSpec(memory_space=pl.ANY), vmem, vmem,
        ],
        out_specs=vmem,
        scratch_shapes=[
            pltpu.VMEM((4, 512, 128), jnp.float32),
            pltpu.VMEM((512, 512), jnp.bfloat16),
            pltpu.VMEM((512, 512), jnp.bfloat16),
            pltpu.VMEM((256, 512), jnp.float32),
            pltpu.VMEM((1024, 4096), jnp.bfloat16),
            pltpu.VMEM((768, 4096), jnp.bfloat16),
            pltpu.VMEM((768, 1024), jnp.bfloat16),
            pltpu.VMEM((8, 768, 512), jnp.bfloat16),
            pltpu.VMEM((7, 384, 512), jnp.bfloat16),
            pltpu.VMEM((7, 384, 512), jnp.bfloat16),
            pltpu.SemaphoreType.DMA,
            pltpu.SemaphoreType.DMA,
            pltpu.SemaphoreType.DMA,
            pltpu.SemaphoreType.DMA,
            pltpu.SemaphoreType.DMA((40,)),
            pltpu.SemaphoreType.DMA((32,)),
            pltpu.SemaphoreType.DMA((32,)),
            pltpu.SemaphoreType.DMA((2, 7)),
            pltpu.SemaphoreType.DMA((2, 7)),
        ],
        compiler_params=pltpu.CompilerParams(
            collective_id=0, has_side_effects=True, vmem_limit_bytes=56 * 1024 * 1024
        ),
    )
    return call(
        sample_rows.reshape(32, 32), buffer, window,
        enc_scale.reshape(1, 1024), dec_bias.reshape(1, 4096),
    )


def solution(mesh):
    in_specs = (P("buf", None), P("lat"), P("buf", None), P("lat"), P())
    out_specs = P("buf", "lat")
    return jax.shard_map(
        on_device, mesh=mesh, in_specs=in_specs, out_specs=out_specs, check_vma=False
    )
```

```python
import jax
import jax.numpy as jnp
from jax import lax
from jax.experimental import pallas as pl
from jax.experimental.pallas import tpu as pltpu
from jax.sharding import PartitionSpec as P

MESH = pl.DeviceIdType.MESH
NT = (((1,), (1,)), ((), ()))
ONE = 384
HALF = ONE // 2
SUB = 48


def rem(value, size):
    return lax.rem(value, size)


def fused(
    rows_ref, buf_hbm, win_hbm, scale_ref, bias_ref, out_ref,
    buf, stage, send, recv, picked, units, cen, cen_pair, act, act_pair,
    part, flow_r, flow_l, part_pair, pair_r, pair_l, scale_pair,
    in_sem, own_sem, a2a_send, a2a_recv, z_send, z_recv, ag_send, ag_recv, ag_recv2,
    rs_send, rs_recv, pair_send, pair_recv,
):
    me = lax.axis_index("buf")
    owner = lax.axis_index("lat")
    core = rem(me, 2)
    chip = me // 2
    x, y = chip // 4, rem(chip, 4)
    a = x + core * (y - x)
    b = y + core * (x - y)
    right, left, opposite = rem(owner + 1, 8), rem(owner + 7, 8), rem(owner + 4, 8)

    barrier = pltpu.get_barrier_semaphore()

    def greet(k, carry):
        pl.semaphore_signal(
            barrier, inc=1, device_id={"buf": rem(me + k, 32)}, device_id_type=MESH
        )
        return carry

    lax.fori_loop(1, 32, greet, 0)
    for near in (right, left, opposite):
        pl.semaphore_signal(barrier, inc=1, device_id={"lat": near}, device_id_type=MESH)

    buf_copy = pltpu.make_async_copy(buf_hbm, buf, own_sem)
    buf_copy.start()
    loads = [pltpu.make_async_copy(win_hbm.at[pl.ds(0, ONE), :], cen, in_sem.at[4])]
    for p in range(4):
        low = pl.multiple_of(ONE + rem(owner + 8 - p, 8) * SUB, 16)
        loads.append(pltpu.make_async_copy(
            win_hbm.at[pl.ds(low, SUB), :], cen_pair.at[pl.ds(p * SUB, SUB), :], in_sem.at[p]
        ))
    for load in loads:
        load.start()

    rows = rows_ref[...]
    offset = rows - me * 256
    mine = (offset >= 0) & (offset < 256)
    lanes = lax.broadcasted_iota(jnp.int32, (8, 128), 1)
    key = (lanes * 256 + offset).astype(jnp.float32)
    first, last = [], []
    for g in range(4):
        here = mine & (lanes >= g * 32) & (lanes < g * 32 + 32)
        first.append(jnp.min(jnp.where(here, key, 32767.0), axis=1, keepdims=True))
        last.append(jnp.max(jnp.where(here, key, 0.0), axis=1, keepdims=True))
    chosen = jnp.concatenate(first + last, axis=0).astype(jnp.int32)
    hot = jnp.bitwise_and(chosen, 255) == lax.broadcasted_iota(jnp.int32, (64, 256), 1)
    hot = hot.astype(jnp.float32).astype(jnp.bfloat16)
    buf_copy.wait()
    for q in range(8):
        piece = jnp.dot(
            hot, buf[:, q * 512:(q + 1) * 512], preferred_element_type=jnp.float32
        )
        for r in range(2):
            for g in range(4):
                stage[g, pl.ds(r * 8 + q, 32, stride=16), :] = (
                    piece[r * 32:r * 32 + 32, g * 128:(g + 1) * 128]
                )
    for g in range(4):
        send[:, g * 128:(g + 1) * 128] = stage[g].astype(jnp.bfloat16)

    pl.semaphore_wait(barrier, 34)

    def block_of(device):
        dc = rem(device, 2)
        dchip = device // 2
        dx, dy = dchip // 4, rem(dchip, 4)
        return dc * 16 + (dy + dc * (dx - dy)) * 4 + dx + dc * (dy - dx)

    def tile16(ref, index):
        return ref.at[pl.ds(pl.multiple_of(index * 16, 16), 16), :]

    def place(block):
        return rem(block, 4) * 8 + block // 4

    def push(k, carry):
        target = rem(me + k, 32)
        pltpu.make_async_remote_copy(
            src_ref=tile16(send, place(block_of(target))),
            dst_ref=tile16(recv, me),
            send_sem=a2a_send,
            recv_sem=a2a_recv,
            device_id={"buf": target},
            device_id_type=MESH,
        ).start()
        return carry

    lax.fori_loop(1, 32, push, 0)
    my_block = core * 16 + b * 4 + a
    own_copy = pltpu.make_async_copy(tile16(send, place(my_block)), tile16(recv, me), own_sem)
    own_copy.start()
    scale_copy = pltpu.make_async_remote_copy(
        src_ref=scale_ref, dst_ref=scale_pair, send_sem=z_send.at[0], recv_sem=z_recv.at[0],
        device_id={"lat": opposite}, device_id_type=MESH,
    )
    scale_copy.start()

    for load in loads:
        load.wait()

    def center(t, carry):
        at = pl.ds(pl.multiple_of(t * 32, 32), 32)
        cen[at, :] = (cen[at, :].astype(jnp.float32) - bias_ref[...]).astype(jnp.bfloat16)
        return carry

    def center_pair(t, carry):
        at = pl.ds(pl.multiple_of(t * 32, 32), 32)
        cen_pair[at, :] = (
            cen_pair[at, :].astype(jnp.float32) - bias_ref[...]
        ).astype(jnp.bfloat16)
        return carry

    lax.fori_loop(0, ONE // 32, center, 0)
    lax.fori_loop(0, 4 * SUB // 32, center_pair, 0)

    own_copy.wait()
    pltpu.make_async_copy(recv.at[pl.ds(0, 496), :], recv.at[pl.ds(0, 496), :], a2a_recv).wait()

    own = jnp.broadcast_to(rows_ref[pl.ds(my_block // 4, 1), :], (32, 128))
    own = lax.shift_right_logical(own, 8).astype(jnp.float32)
    entry = lax.broadcasted_iota(jnp.int32, (32, 128), 0)
    peer = lax.broadcasted_iota(jnp.int32, (32, 128), 1) - rem(my_block, 4) * 32
    source = jnp.sum(jnp.where(entry == peer, own, 0.0), axis=1, keepdims=True)
    twin = (own == source) & (peer >= 0) & (peer < entry)
    rank = jnp.sum(jnp.where(twin, 1.0, 0.0), axis=1, keepdims=True)
    code = (source * 16.0 + rank * 8.0).astype(jnp.int32)
    code = jnp.concatenate([code + q for q in range(8)], axis=0)
    hot = code == lax.broadcasted_iota(jnp.int32, (256, 512), 1)
    hot = hot.astype(jnp.float32).astype(jnp.bfloat16)
    picked[...] = jnp.dot(hot, recv[...], preferred_element_type=jnp.float32)
    squares = jnp.zeros((32, 512), jnp.float32)
    for q in range(8):
        value = picked[q * 32:q * 32 + 32, :]
        squares += value * value
    inverse = lax.rsqrt(jnp.sum(squares, axis=1, keepdims=True) + 1e-06)
    mine_at = pl.ds(pl.multiple_of(my_block * 32, 32), 32)
    for q in range(8):
        value = picked[q * 32:q * 32 + 32, :]
        units[0, mine_at, q * 512:q * 512 + 512] = (value * inverse).astype(jnp.bfloat16)

    def block_at(da, db):
        return core * 16 + rem(b + db + 4, 4) * 4 + rem(a + da + 4, 4)

    def device_at(da, db):
        pa, pb = rem(a + da + 4, 4), rem(b + db + 4, 4)
        px, py = pa + core * (pb - pa), pb + core * (pa - pb)
        return (px * 4 + py) * 2 + core

    sibling = me + 1 - 2 * core
    sent = [[], []]

    def block_ref(w, block, count=32, half=0):
        return units.at[w, pl.ds(pl.multiple_of(block * 32 + half * 16, 16), count), :]

    def give(w, block, target, count=32, half=0):
        at = block_ref(w, block, count, half)
        sem = ag_recv2 if half else ag_recv
        copy = pltpu.make_async_remote_copy(
            src_ref=at, dst_ref=at, send_sem=ag_send.at[w, len(sent[w])],
            recv_sem=sem.at[w, block], device_id={"buf": target}, device_id_type=MESH,
        )
        copy.start()
        sent[w].append(copy)

    def arrive(w, block, count=32, half=0):
        at = block_ref(w, block, count, half)
        sem = ag_recv2 if half else ag_recv
        pltpu.make_async_copy(at, at, sem.at[w, block]).wait()

    def spread(w, block):
        give(w, block, device_at(0, 1))
        give(w, block, device_at(0, -1))
        give(w, block, sibling)

    def second(w, da):
        block = block_at(da, -1)
        arrive(w, block)
        give(w, block, device_at(0, 1), 16, 0)
        give(w, block, sibling)
        block = block_at(da, 1)
        arrive(w, block)
        give(w, block, device_at(0, -1), 16, 1)
        give(w, block, sibling)

    def far(w, da):
        block = block_at(da, 2)
        arrive(w, block, 16, 0)
        arrive(w, block, 16, 1)
        give(w, block, sibling)

    def step(w, n):
        if n == 0:
            give(w, my_block, device_at(1, 0))
            give(w, my_block, device_at(-1, 0))
            spread(w, my_block)
        elif n == 1:
            block = block_at(-1, 0)
            arrive(w, block)
            give(w, block, device_at(1, 0), 16, 0)
            spread(w, block)
        elif n == 2:
            block = block_at(1, 0)
            arrive(w, block)
            give(w, block, device_at(-1, 0), 16, 1)
            spread(w, block)
        elif n == 3:
            second(w, 0)
        elif n == 4:
            block = block_at(2, 0)
            arrive(w, block, 16, 0)
            arrive(w, block, 16, 1)
            spread(w, block)
        elif n < 8:
            second(w, (-1, 1, 2)[n - 5])
        else:
            far(w, (0, -1, 1, 2)[n - 8])

    step(0, 0)
    z_copy = pltpu.make_async_remote_copy(
        src_ref=block_ref(0, my_block), dst_ref=block_ref(1, my_block),
        send_sem=z_send.at[1], recv_sem=z_recv.at[1],
        device_id={"lat": opposite}, device_id_type=MESH,
    )
    z_copy.start()
    for n in range(1, 8):
        step(0, n)

    def encode(group):
        at = pl.ds(pl.multiple_of(group * 256, 256), 256)
        scores = lax.dot_general(
            cen[...], units[0, at, :], NT, preferred_element_type=jnp.float32
        )
        act[:, at] = jnp.maximum(scores * scale_ref[:, at], 0.0).astype(jnp.bfloat16)

    def encode_pair(w, group):
        at = pl.ds(pl.multiple_of(group * 256, 256), 256)
        scale = (scale_pair if w else scale_ref)[:, at]
        scores = lax.dot_general(
            cen_pair[...], units[w, at, :], NT, preferred_element_type=jnp.float32
        )
        act_pair[w, :, at] = jnp.maximum(scores * scale, 0.0).astype(jnp.bfloat16)

    other = 1 - core
    other_b = x + core * (y - x)
    mine_near = core * 2 + b // 2
    mine_far = core * 2 + 1 - b // 2
    other_near = other * 2 + other_b // 2
    other_far = other * 2 + 1 - other_b // 2

    def arrive_group(w, group):
        def one(i, carry):
            arrive(w, group * 8 + i)
            return carry

        lax.fori_loop(0, 8, one, 0)

    encode(mine_near)
    for n in range(8, 12):
        step(0, n)
    arrive_group(0, other_near)
    encode(other_near)
    encode(mine_far)
    arrive_group(0, other_far)
    encode(other_far)

    def decode(target):
        columns = pl.ds(pl.multiple_of(target * 512, 512), 512)
        value = jnp.dot(act[...], units[0, :, columns], preferred_element_type=jnp.float32)
        part[target] = value.astype(jnp.bfloat16)

    def half_of(ref, half):
        return ref.at[pl.ds(half * HALF, HALF), :]

    def rs_copy(i, source, flow, way):
        return pltpu.make_async_remote_copy(
            src_ref=source, dst_ref=flow.at[i],
            send_sem=rs_send.at[way, i], recv_sem=rs_recv.at[way, i],
            device_id={"lat": left if way else right}, device_id_type=MESH,
        )

    def rs_wait(i, flow, way):
        pltpu.make_async_copy(flow.at[i], flow.at[i], rs_recv.at[way, i]).wait()

    def hop(i):
        for way, flow in ((0, flow_r), (1, flow_l)):
            low = ((i + way) % 2) * HALF
            away = 4 - (i + 1) // 2
            target = rem(owner + (8 - away if way else away), 8)
            rs_wait(i - 2, flow, way)
            total = flow[i - 2].astype(jnp.float32)
            total += part[target, low:low + HALF, :].astype(jnp.float32)
            flow[i - 2] = total.astype(jnp.bfloat16)
            rs_copy(i, flow.at[i - 2], flow, way).start()

    decode(opposite)
    rs_copy(0, half_of(part.at[opposite], 0), flow_r, 0).start()
    rs_copy(0, half_of(part.at[opposite], 1), flow_l, 1).start()
    z_copy.wait_recv()
    step(1, 0)

    def decode_next(i, carry):
        decode(rem(owner + 3 + 2 * i, 8))
        return carry

    lax.fori_loop(0, 2, decode_next, 0)
    rs_copy(1, half_of(part.at[rem(owner + 3, 8)], 1), flow_r, 0).start()
    rs_copy(1, half_of(part.at[rem(owner + 5, 8)], 0), flow_l, 1).start()
    step(1, 1)
    step(1, 2)

    def decode_rest(i, carry):
        decode(rem(owner + 6 + i, 8))
        return carry

    lax.fori_loop(0, 5, decode_rest, 0)
    step(1, 3)
    hop(2)
    step(1, 4)
    step(1, 5)
    lax.fori_loop(0, 4, lambda i, carry: (encode_pair(0, i), carry)[1], 0)
    hop(3)
    step(1, 6)
    step(1, 7)
    scale_copy.wait_recv()
    encode_pair(1, mine_near)
    hop(4)
    for n in range(8, 12):
        step(1, n)
    arrive_group(1, other_near)
    encode_pair(1, other_near)
    encode_pair(1, mine_far)
    hop(5)
    arrive_group(1, other_far)
    encode_pair(1, other_far)
    hop(6)

    def decode_pair(o, carry):
        columns = pl.ds(pl.multiple_of(rem(owner + o, 8) * 512, 512), 512)
        value = jnp.dot(act_pair[0], units[0, :, columns], preferred_element_type=jnp.float32)
        value += jnp.dot(act_pair[1], units[1, :, columns], preferred_element_type=jnp.float32)
        value = value.astype(jnp.bfloat16)
        for p in range(4):
            part_pair[p, o] = value[p * SUB:(p + 1) * SUB, :]
        return carry

    def pair_copy(way, p, source):
        flow = pair_l if way else pair_r
        return pltpu.make_async_remote_copy(
            src_ref=source, dst_ref=flow.at[p, pl.ds(0, 5 - p)],
            send_sem=pair_send.at[way, p], recv_sem=pair_recv.at[way, p],
            device_id={"lat": left if way else right}, device_id_type=MESH,
        )

    def pair_wait(way, p):
        flow = pair_l if way else pair_r
        at = flow.at[p, pl.ds(0, 5 - p)]
        pltpu.make_async_copy(at, at, pair_recv.at[way, p]).wait()

    lax.fori_loop(1, 8, decode_pair, 0)
    pair_copies = [pair_copy(0, 0, part_pair.at[0, pl.ds(1, 5)])]
    pair_copies.append(pair_copy(1, 0, part_pair.at[3, pl.ds(3, 5)]))
    for copy in pair_copies:
        copy.start()
    decode_pair(0, 0)

    bias = bias_ref[:, pl.ds(pl.multiple_of(owner * 512, 512), 512)]
    for i in (5, 6):
        rs_wait(i, flow_r, 0)
        rs_wait(i, flow_l, 1)
    for half in range(2):
        at = slice(half * HALF, half * HALF + HALF)
        total = part[owner, at, :].astype(jnp.float32) + bias
        total += flow_r[6 - half].astype(jnp.float32) + flow_l[5 + half].astype(jnp.float32)
        out_ref[at, :] = total.astype(jnp.bfloat16)

    for p in range(1, 5):
        for way, flow in ((0, pair_r), (1, pair_l)):
            pair_wait(way, p - 1)
            low = 0 if way else 1
            if p < 4:
                for k in range(5 - p):
                    mine_part = part_pair[3 - p, 3 + p + k] if way else part_pair[p, 1 + k]
                    total = flow[p - 1, low + k].astype(jnp.float32)
                    total += mine_part.astype(jnp.float32)
                    flow[p - 1, low + k] = total.astype(jnp.bfloat16)
            copy = pair_copy(way, p, flow.at[p - 1, pl.ds(low, 5 - p)])
            copy.start()
            pair_copies.append(copy)
    for way in range(2):
        pair_wait(way, 4)

    for r in range(-4, 4):
        terms = []
        if -3 <= r <= 0:
            terms.append(part_pair[-r, 0])
        for p in range(5):
            if (r + 1 + p) % 8 == 0:
                terms.append(pair_r[p, 0])
            if (r + 2 - p) % 8 == 0:
                terms.append(pair_l[p, 4 - p])
        total = jnp.broadcast_to(bias, (SUB, 512))
        for term in terms:
            total += term.astype(jnp.float32)
        low = pl.multiple_of(ONE + rem(owner + 8 + r, 8) * SUB, 16)
        out_ref[pl.ds(low, SUB), :] = total.astype(jnp.bfloat16)

    pltpu.make_async_copy(send.at[pl.ds(0, 496), :], send.at[pl.ds(0, 496), :], a2a_send).wait()
    for copy in [scale_copy, z_copy] + sent[0] + sent[1] + pair_copies:
        copy.wait_send()

    def drain(i, carry):
        for way in range(2):
            pltpu.make_async_copy(flow_r.at[i], flow_r.at[i], rs_send.at[way, i]).wait()
        return carry

    lax.fori_loop(0, 7, drain, 0)


def on_device(buffer, sample_rows, window, enc_scale, dec_bias):
    vmem = pl.BlockSpec(memory_space=pltpu.VMEM)
    anywhere = pl.BlockSpec(memory_space=pl.ANY)
    call = pl.pallas_call(
        fused,
        out_shape=jax.ShapeDtypeStruct((768, 512), jnp.bfloat16),
        in_specs=[vmem, anywhere, anywhere, vmem, vmem],
        out_specs=vmem,
        scratch_shapes=[
            pltpu.VMEM((256, 4096), jnp.bfloat16),
            pltpu.VMEM((4, 512, 128), jnp.float32),
            pltpu.VMEM((512, 512), jnp.bfloat16),
            pltpu.VMEM((512, 512), jnp.bfloat16),
            pltpu.VMEM((256, 512), jnp.float32),
            pltpu.VMEM((2, 1024, 4096), jnp.bfloat16),
            pltpu.VMEM((ONE, 4096), jnp.bfloat16),
            pltpu.VMEM((4 * SUB, 4096), jnp.bfloat16),
            pltpu.VMEM((ONE, 1024), jnp.bfloat16),
            pltpu.VMEM((2, 4 * SUB, 1024), jnp.bfloat16),
            pltpu.VMEM((8, ONE, 512), jnp.bfloat16),
            pltpu.VMEM((7, HALF, 512), jnp.bfloat16),
            pltpu.VMEM((7, HALF, 512), jnp.bfloat16),
            pltpu.VMEM((4, 8, SUB, 512), jnp.bfloat16),
            pltpu.VMEM((5, 5, SUB, 512), jnp.bfloat16),
            pltpu.VMEM((5, 5, SUB, 512), jnp.bfloat16),
            pltpu.VMEM((1, 1024), jnp.float32),
            pltpu.SemaphoreType.DMA((5,)),
            pltpu.SemaphoreType.DMA,
            pltpu.SemaphoreType.DMA,
            pltpu.SemaphoreType.DMA,
            pltpu.SemaphoreType.DMA((2,)),
            pltpu.SemaphoreType.DMA((2,)),
            pltpu.SemaphoreType.DMA((2, 40)),
            pltpu.SemaphoreType.DMA((2, 32)),
            pltpu.SemaphoreType.DMA((2, 32)),
            pltpu.SemaphoreType.DMA((2, 7)),
            pltpu.SemaphoreType.DMA((2, 7)),
            pltpu.SemaphoreType.DMA((2, 5)),
            pltpu.SemaphoreType.DMA((2, 5)),
        ],
        compiler_params=pltpu.CompilerParams(
            collective_id=0, has_side_effects=True, vmem_limit_bytes=56 * 1024 * 1024
        ),
    )
    return call(
        sample_rows.reshape(8, 128), buffer, window,
        enc_scale.reshape(1, 1024), dec_bias.reshape(1, 4096),
    )


def solution(mesh):
    in_specs = (P("buf", None), P("lat"), P("buf", None), P("lat"), P())
    out_specs = P("buf", "lat")
    return jax.shard_map(
        on_device, mesh=mesh, in_specs=in_specs, out_specs=out_specs, check_vma=False
    )
```

```python
import jax
import jax.numpy as jnp
from jax import lax
from jax.experimental import pallas as pl
from jax.experimental.pallas import tpu as pltpu
from jax.sharding import PartitionSpec as P

MESH = pl.DeviceIdType.MESH
NT = (((1,), (1,)), ((), ()))
ONE = 384
HALF = ONE // 2
PIECES = 3
SUB = 16 * PIECES


def rem(value, size):
    return lax.rem(value, size)


def fused(
    rows_ref, buf_hbm, win_hbm, scale_ref, bias_ref, out_ref,
    buf, stage, send, recv, picked, units, cen, cen_pair, act, act_pair,
    part, flow_r, flow_l, part_pair, pair_flow, pair_far, scale_pair,
    in_sem, own_sem, a2a_send, a2a_recv, z_send, z_recv, ag_send, ag_recv,
    rs_send, rs_recv, pair_send, pair_recv,
):
    me = lax.axis_index("buf")
    owner = lax.axis_index("lat")
    core = rem(me, 2)
    chip = me // 2
    x, y = chip // 4, rem(chip, 4)
    a = x + core * (y - x)
    b = y + core * (x - y)
    right, left, opposite = rem(owner + 1, 8), rem(owner + 7, 8), rem(owner + 4, 8)

    barrier = pltpu.get_barrier_semaphore()

    def greet(k, carry):
        pl.semaphore_signal(
            barrier, inc=1, device_id={"buf": rem(me + k, 32)}, device_id_type=MESH
        )
        return carry

    lax.fori_loop(1, 32, greet, 0)
    for k in (1, 2, 4, 6, 7):
        pl.semaphore_signal(barrier, inc=1, device_id={"lat": rem(owner + k, 8)}, device_id_type=MESH)

    buf_copy = pltpu.make_async_copy(buf_hbm, buf, own_sem)
    buf_copy.start()
    loads = [pltpu.make_async_copy(win_hbm.at[pl.ds(0, ONE), :], cen, in_sem.at[4])]
    for p in range(4):
        low = pl.multiple_of(ONE + rem(owner + 8 - p, 8) * SUB, 16)
        loads.append(pltpu.make_async_copy(
            win_hbm.at[pl.ds(low, SUB), :], cen_pair.at[pl.ds(p * SUB, SUB), :], in_sem.at[p]
        ))
    for load in loads:
        load.start()

    rows = rows_ref[...]
    offset = rows - me * 256
    mine = (offset >= 0) & (offset < 256)
    lanes = lax.broadcasted_iota(jnp.int32, (8, 128), 1)
    key = (lanes * 256 + offset).astype(jnp.float32)
    first, last = [], []
    for g in range(4):
        here = mine & (lanes >= g * 32) & (lanes < g * 32 + 32)
        first.append(jnp.min(jnp.where(here, key, 32767.0), axis=1, keepdims=True))
        last.append(jnp.max(jnp.where(here, key, 0.0), axis=1, keepdims=True))
    chosen = jnp.concatenate(first + last, axis=0).astype(jnp.int32)
    hot = jnp.bitwise_and(chosen, 255) == lax.broadcasted_iota(jnp.int32, (64, 256), 1)
    hot = hot.astype(jnp.float32).astype(jnp.bfloat16)
    buf_copy.wait()
    for q in range(8):
        piece = jnp.dot(
            hot, buf[:, q * 512:(q + 1) * 512], preferred_element_type=jnp.float32
        )
        for r in range(2):
            for g in range(4):
                stage[g, pl.ds(r * 8 + q, 32, stride=16), :] = (
                    piece[r * 32:r * 32 + 32, g * 128:(g + 1) * 128]
                )
    for g in range(4):
        send[:, g * 128:(g + 1) * 128] = stage[g].astype(jnp.bfloat16)

    pl.semaphore_wait(barrier, 36)

    def block_of(device):
        dc = rem(device, 2)
        dchip = device // 2
        dx, dy = dchip // 4, rem(dchip, 4)
        return dc * 16 + (dx + dc * (dy - dx)) * 4 + dy + dc * (dx - dy)

    def tile16(ref, index):
        return ref.at[pl.ds(pl.multiple_of(index * 16, 16), 16), :]

    def place(block):
        return rem(block, 4) * 8 + block // 4

    def push(k, carry):
        far = 32 - k
        tx, ty = rem(x + far // 8, 4), rem(y + rem(far, 8) // 2, 4)
        target = (tx * 4 + ty) * 2 + rem(core + far, 2)
        pltpu.make_async_remote_copy(
            src_ref=tile16(send, place(block_of(target))),
            dst_ref=tile16(recv, me),
            send_sem=a2a_send,
            recv_sem=a2a_recv,
            device_id={"buf": target},
            device_id_type=MESH,
        ).start()
        return carry

    lax.fori_loop(1, 32, push, 0)
    my_block = core * 16 + a * 4 + b
    own_copy = pltpu.make_async_copy(tile16(send, place(my_block)), tile16(recv, me), own_sem)
    own_copy.start()
    scale_copy = pltpu.make_async_remote_copy(
        src_ref=scale_ref, dst_ref=scale_pair, send_sem=z_send.at[0], recv_sem=z_recv.at[0],
        device_id={"lat": opposite}, device_id_type=MESH,
    )
    scale_copy.start()

    for load in loads:
        load.wait()

    def center(t, carry):
        at = pl.ds(pl.multiple_of(t * 32, 32), 32)
        cen[at, :] = (cen[at, :].astype(jnp.float32) - bias_ref[...]).astype(jnp.bfloat16)
        return carry

    def center_pair(t, carry):
        at = pl.ds(pl.multiple_of(t * 32, 32), 32)
        cen_pair[at, :] = (
            cen_pair[at, :].astype(jnp.float32) - bias_ref[...]
        ).astype(jnp.bfloat16)
        return carry

    lax.fori_loop(0, ONE // 32, center, 0)
    lax.fori_loop(0, 4 * SUB // 32, center_pair, 0)

    own_copy.wait()
    pltpu.make_async_copy(recv.at[pl.ds(0, 496), :], recv.at[pl.ds(0, 496), :], a2a_recv).wait()

    own = jnp.broadcast_to(rows_ref[pl.ds(my_block // 4, 1), :], (32, 128))
    own = lax.shift_right_logical(own, 8).astype(jnp.float32)
    entry = lax.broadcasted_iota(jnp.int32, (32, 128), 0)
    peer = lax.broadcasted_iota(jnp.int32, (32, 128), 1) - rem(my_block, 4) * 32
    source = jnp.sum(jnp.where(entry == peer, own, 0.0), axis=1, keepdims=True)
    twin = (own == source) & (peer >= 0) & (peer < entry)
    rank = jnp.sum(jnp.where(twin, 1.0, 0.0), axis=1, keepdims=True)
    code = (source * 16.0 + rank * 8.0).astype(jnp.int32)
    code = jnp.concatenate([code + q for q in range(8)], axis=0)
    hot = code == lax.broadcasted_iota(jnp.int32, (256, 512), 1)
    hot = hot.astype(jnp.float32).astype(jnp.bfloat16)
    picked[...] = jnp.dot(hot, recv[...], preferred_element_type=jnp.float32)
    squares = jnp.zeros((32, 512), jnp.float32)
    for q in range(8):
        value = picked[q * 32:q * 32 + 32, :]
        squares += value * value
    inverse = lax.rsqrt(jnp.sum(squares, axis=1, keepdims=True) + 1e-06)
    mine_at = pl.ds(pl.multiple_of(my_block * 32, 32), 32)
    for q in range(8):
        value = picked[q * 32:q * 32 + 32, :]
        units[0, mine_at, q * 512:q * 512 + 512] = (value * inverse).astype(jnp.bfloat16)

    def block_at(da, db):
        return core * 16 + rem(a + da + 4, 4) * 4 + rem(b + db + 4, 4)

    def device_at(da, db):
        pa, pb = rem(a + da + 4, 4), rem(b + db + 4, 4)
        px, py = pa + core * (pb - pa), pb + core * (pa - pb)
        return (px * 4 + py) * 2 + core

    sibling = me + 1 - 2 * core
    sent = [[], []]

    mate = 1 - 2 * rem(a, 2)

    def block_ref(w, block):
        return units.at[w, pl.ds(pl.multiple_of(block * 32, 32), 32), :]

    def give(w, block, target):
        at = block_ref(w, block)
        copy = pltpu.make_async_remote_copy(
            src_ref=at, dst_ref=at, send_sem=ag_send.at[w, len(sent[w])],
            recv_sem=ag_recv.at[w, block], device_id={"buf": target}, device_id_type=MESH,
        )
        copy.start()
        sent[w].append(copy)

    def arrive(w, block):
        at = block_ref(w, block)
        pltpu.make_async_copy(at, at, ag_recv.at[w, block]).wait()

    def spread(w, block):
        for db in (2, 1, -1):
            give(w, block, device_at(0, db))
        give(w, block, sibling)

    def step(w, n):
        da = (0, mate, -mate, 2)[n % 4]
        if n == 0:
            for da in (mate, 2, -mate):
                give(w, my_block, device_at(da, 0))
            spread(w, my_block)
        elif n < 4:
            block = block_at(da, 0)
            arrive(w, block)
            spread(w, block)
        else:
            for db in (1, -1, 2):
                block = block_at(da, db)
                arrive(w, block)
                give(w, block, sibling)

    step(0, 0)
    z_copy = pltpu.make_async_remote_copy(
        src_ref=block_ref(0, my_block), dst_ref=block_ref(1, my_block),
        send_sem=z_send.at[1], recv_sem=z_recv.at[1],
        device_id={"lat": opposite}, device_id_type=MESH,
    )
    z_copy.start()
    for n in range(1, 6):
        step(0, n)

    def encode(group):
        at = pl.ds(pl.multiple_of(group * 256, 256), 256)
        scores = lax.dot_general(
            cen[...], units[0, at, :], NT, preferred_element_type=jnp.float32
        )
        act[:, at] = jnp.maximum(scores * scale_ref[:, at], 0.0).astype(jnp.bfloat16)

    def encode_pair(w, group):
        at = pl.ds(pl.multiple_of(group * 256, 256), 256)
        scale = (scale_pair if w else scale_ref)[:, at]
        scores = lax.dot_general(
            cen_pair[...], units[w, at, :], NT, preferred_element_type=jnp.float32
        )
        act_pair[w, :, at] = jnp.maximum(scores * scale, 0.0).astype(jnp.bfloat16)

    other = 1 - core
    other_a = y + core * (x - y)
    mine_near = core * 2 + a // 2
    mine_far = core * 2 + 1 - a // 2
    other_near = other * 2 + other_a // 2
    other_far = other * 2 + 1 - other_a // 2

    def arrive_group(w, group):
        def one(i, carry):
            arrive(w, group * 8 + i)
            return carry

        lax.fori_loop(0, 8, one, 0)

    encode(mine_near)
    step(0, 6)
    arrive_group(0, other_near)
    encode(other_near)
    step(0, 7)
    z_copy.wait_recv()
    step(1, 0)
    encode(mine_far)
    arrive_group(0, other_far)
    encode(other_far)

    def decode(target):
        columns = pl.ds(pl.multiple_of(target * 512, 512), 512)
        value = jnp.dot(act[...], units[0, :, columns], preferred_element_type=jnp.float32)
        part[target] = value.astype(jnp.bfloat16)

    def half_of(ref, half):
        return ref.at[pl.ds(half * HALF, HALF), :]

    def rs_copy(i, source, flow, way):
        return pltpu.make_async_remote_copy(
            src_ref=source, dst_ref=flow.at[i],
            send_sem=rs_send.at[way, i], recv_sem=rs_recv.at[way, i],
            device_id={"lat": left if way else right}, device_id_type=MESH,
        )

    def rs_wait(i, flow, way):
        pltpu.make_async_copy(flow.at[i], flow.at[i], rs_recv.at[way, i]).wait()

    def hop(i):
        for way, flow in ((0, flow_r), (1, flow_l)):
            low = ((i + way) % 2) * HALF
            away = 4 - (i + 1) // 2
            target = rem(owner + (8 - away if way else away), 8)
            rs_wait(i - 2, flow, way)
            total = flow[i - 2].astype(jnp.float32)
            total += part[target, low:low + HALF, :].astype(jnp.float32)
            flow[i - 2] = total.astype(jnp.bfloat16)
            rs_copy(i, flow.at[i - 2], flow, way).start()

    decode(opposite)
    rs_copy(0, half_of(part.at[opposite], 0), flow_r, 0).start()
    rs_copy(0, half_of(part.at[opposite], 1), flow_l, 1).start()

    def decode_next(i, carry):
        decode(rem(owner + 3 + 2 * i, 8))
        return carry

    lax.fori_loop(0, 2, decode_next, 0)
    rs_copy(1, half_of(part.at[rem(owner + 3, 8)], 1), flow_r, 0).start()
    rs_copy(1, half_of(part.at[rem(owner + 5, 8)], 0), flow_l, 1).start()
    for n in range(1, 4):
        step(1, n)

    def decode_rest(i, carry):
        decode(rem(owner + 6 + i, 8))
        return carry

    lax.fori_loop(0, 5, decode_rest, 0)
    step(1, 4)
    hop(2)
    lax.fori_loop(0, 4, lambda i, carry: (encode_pair(0, i), carry)[1], 0)
    step(1, 5)
    hop(3)
    scale_copy.wait_recv()
    encode_pair(1, mine_near)
    hop(4)
    step(1, 6)
    arrive_group(1, other_near)
    encode_pair(1, other_near)
    hop(5)
    step(1, 7)
    encode_pair(1, mine_far)
    arrive_group(1, other_far)
    encode_pair(1, other_far)
    hop(6)

    def decode_pair(o, carry):
        columns = pl.ds(pl.multiple_of(rem(owner + o, 8) * 512, 512), 512)
        value = jnp.dot(act_pair[0], units[0, :, columns], preferred_element_type=jnp.float32)
        value += jnp.dot(act_pair[1], units[1, :, columns], preferred_element_type=jnp.float32)
        value = value.astype(jnp.bfloat16)
        for p in range(4):
            for c in range(PIECES):
                low = p * SUB + c * 16
                part_pair[c, p, o] = value[low:low + 16, :]
        return carry

    pair_copies = []

    def pair_give(way, c, p, source, dest, distance=1, slot=None):
        slot = p if slot is None else slot
        copy = pltpu.make_async_remote_copy(
            src_ref=source, dst_ref=dest,
            send_sem=pair_send.at[way, c, slot], recv_sem=pair_recv.at[way, c, slot],
            device_id={"lat": rem(owner + (8 - distance if way else distance), 8)},
            device_id_type=MESH,
        )
        copy.start()
        pair_copies.append(copy)

    def pair_wait(way, c, p):
        if p == 4:
            at = pair_far.at[way, c]
        else:
            at = pair_flow.at[way, c, p, pl.ds(0, 5 - p if p < 3 else 1)]
        pltpu.make_async_copy(at, at, pair_recv.at[way, c, p]).wait()

    lax.fori_loop(1, 8, decode_pair, 0)
    for c in range(PIECES):
        for way in range(2):
            source = part_pair.at[c, 3 if way else 0, pl.ds(3 if way else 1, 5)]
            pair_give(way, c, 0, source, pair_flow.at[way, c, 0])
    decode_pair(0, 0)

    bias = bias_ref[:, pl.ds(pl.multiple_of(owner * 512, 512), 512)]

    def finish_one():
        for i in (5, 6):
            rs_wait(i, flow_r, 0)
            rs_wait(i, flow_l, 1)
        for half in range(2):
            at = slice(half * HALF, half * HALF + HALF)
            total = part[owner, at, :].astype(jnp.float32) + bias
            total += flow_r[6 - half].astype(jnp.float32) + flow_l[5 + half].astype(jnp.float32)
            out_ref[at, :] = total.astype(jnp.bfloat16)

    for p in range(1, 4):
        for c in range(PIECES):
            for way in range(2):
                pair_wait(way, c, p - 1)
                low = 0 if way else 1
                for k in range(5 - p):
                    mine_part = part_pair[c, 3 - p, 3 + p + k] if way else part_pair[c, p, 1 + k]
                    total = pair_flow[way, c, p - 1, low + k].astype(jnp.float32)
                    total += mine_part.astype(jnp.float32)
                    pair_flow[way, c, p - 1, low + k] = total.astype(jnp.bfloat16)
                source = pair_flow.at[way, c, p - 1, pl.ds(low, 5 - p)]
                if p < 3:
                    pair_give(way, c, p, source, pair_flow.at[way, c, p, pl.ds(0, 5 - p)])
                else:
                    pair_give(way, c, 4, source.at[0 if way else 1], pair_far.at[way, c], 2, 4)
                    pair_give(way, c, 3, source.at[1 if way else 0], pair_flow.at[way, c, 3, 0])
        if p == 1:
            finish_one()
    for c in range(PIECES):
        for way in range(2):
            pair_wait(way, c, 3)
            pair_wait(way, c, 4)

    for c in range(PIECES):
        for r in range(-4, 4):
            terms = []
            if -3 <= r <= 0:
                terms.append(part_pair[c, -r, 0])
            for p in range(4):
                if (r + 1 + p) % 8 == 0:
                    terms.append(pair_flow[0, c, p, 0])
                if (r + 2 - p) % 8 == 0:
                    terms.append(pair_flow[1, c, p, 4 - p if p < 3 else 0])
            if r == 3:
                terms.append(pair_far[0, c])
            if r == 2:
                terms.append(pair_far[1, c])
            total = jnp.broadcast_to(bias, (16, 512))
            for term in terms:
                total += term.astype(jnp.float32)
            low = pl.multiple_of(ONE + rem(owner + 8 + r, 8) * SUB + c * 16, 16)
            out_ref[pl.ds(low, 16), :] = total.astype(jnp.bfloat16)

    pltpu.make_async_copy(send.at[pl.ds(0, 496), :], send.at[pl.ds(0, 496), :], a2a_send).wait()
    for copy in [scale_copy, z_copy] + sent[0] + sent[1] + pair_copies:
        copy.wait_send()

    def drain(i, carry):
        for way in range(2):
            pltpu.make_async_copy(flow_r.at[i], flow_r.at[i], rs_send.at[way, i]).wait()
        return carry

    lax.fori_loop(0, 7, drain, 0)


def on_device(buffer, sample_rows, window, enc_scale, dec_bias):
    vmem = pl.BlockSpec(memory_space=pltpu.VMEM)
    anywhere = pl.BlockSpec(memory_space=pl.ANY)
    call = pl.pallas_call(
        fused,
        out_shape=jax.ShapeDtypeStruct((768, 512), jnp.bfloat16),
        in_specs=[vmem, anywhere, anywhere, vmem, vmem],
        out_specs=vmem,
        scratch_shapes=[
            pltpu.VMEM((256, 4096), jnp.bfloat16),
            pltpu.VMEM((4, 512, 128), jnp.float32),
            pltpu.VMEM((512, 512), jnp.bfloat16),
            pltpu.VMEM((512, 512), jnp.bfloat16),
            pltpu.VMEM((256, 512), jnp.float32),
            pltpu.VMEM((2, 1024, 4096), jnp.bfloat16),
            pltpu.VMEM((ONE, 4096), jnp.bfloat16),
            pltpu.VMEM((4 * SUB, 4096), jnp.bfloat16),
            pltpu.VMEM((ONE, 1024), jnp.bfloat16),
            pltpu.VMEM((2, 4 * SUB, 1024), jnp.bfloat16),
            pltpu.VMEM((8, ONE, 512), jnp.bfloat16),
            pltpu.VMEM((7, HALF, 512), jnp.bfloat16),
            pltpu.VMEM((7, HALF, 512), jnp.bfloat16),
            pltpu.VMEM((PIECES, 4, 8, 16, 512), jnp.bfloat16),
            pltpu.VMEM((2, PIECES, 4, 5, 16, 512), jnp.bfloat16),
            pltpu.VMEM((2, PIECES, 16, 512), jnp.bfloat16),
            pltpu.VMEM((1, 1024), jnp.float32),
            pltpu.SemaphoreType.DMA((5,)),
            pltpu.SemaphoreType.DMA,
            pltpu.SemaphoreType.DMA,
            pltpu.SemaphoreType.DMA,
            pltpu.SemaphoreType.DMA((2,)),
            pltpu.SemaphoreType.DMA((2,)),
            pltpu.SemaphoreType.DMA((2, 40)),
            pltpu.SemaphoreType.DMA((2, 32)),
            pltpu.SemaphoreType.DMA((2, 7)),
            pltpu.SemaphoreType.DMA((2, 7)),
            pltpu.SemaphoreType.DMA((2, PIECES, 5)),
            pltpu.SemaphoreType.DMA((2, PIECES, 5)),
        ],
        compiler_params=pltpu.CompilerParams(
            collective_id=0, has_side_effects=True, vmem_limit_bytes=56 * 1024 * 1024
        ),
    )
    return call(
        sample_rows.reshape(8, 128), buffer, window,
        enc_scale.reshape(1, 1024), dec_bias.reshape(1, 4096),
    )


def solution(mesh):
    in_specs = (P("buf", None), P("lat"), P("buf", None), P("lat"), P())
    out_specs = P("buf", "lat")
    return jax.shard_map(
        on_device, mesh=mesh, in_specs=in_specs, out_specs=out_specs, check_vma=False
    )
```

```python
import jax
import jax.numpy as jnp
from jax import lax
from jax.experimental import pallas as pl
from jax.experimental.pallas import tpu as pltpu
from jax.sharding import PartitionSpec as P

MESH = pl.DeviceIdType.MESH
NT = (((1,), (1,)), ((), ()))
ONE = 384
HALF = ONE // 2
PIECES = 3
SUB = 16 * PIECES


def rem(value, size):
    return lax.rem(value, size)


def fused(
    rows_ref, buf_hbm, win_hbm, scale_ref, bias_ref, out_ref,
    buf, stage, send, recv, picked, units, cen, cen_pair, act, act_pair,
    part, flow_r, flow_l, part_pair, pair_flow, pair_far, scale_pair,
    in_sem, own_sem, a2a_send, a2a_recv, z_send, z_recv, ag_send, ag_recv, ag_recv2,
    rs_send, rs_recv, pair_send, pair_recv,
):
    me = lax.axis_index("buf")
    owner = lax.axis_index("lat")
    core = rem(me, 2)
    chip = me // 2
    x, y = chip // 4, rem(chip, 4)
    a = x + core * (y - x)
    b = y + core * (x - y)
    right, left, opposite = rem(owner + 1, 8), rem(owner + 7, 8), rem(owner + 4, 8)

    barrier = pltpu.get_barrier_semaphore()

    def greet(k, carry):
        pl.semaphore_signal(
            barrier, inc=1, device_id={"buf": rem(me + k, 32)}, device_id_type=MESH
        )
        return carry

    lax.fori_loop(1, 32, greet, 0)
    for k in (1, 2, 4, 6, 7):
        pl.semaphore_signal(barrier, inc=1, device_id={"lat": rem(owner + k, 8)}, device_id_type=MESH)

    buf_copy = pltpu.make_async_copy(buf_hbm, buf, own_sem)
    buf_copy.start()
    loads = [pltpu.make_async_copy(win_hbm.at[pl.ds(0, ONE), :], cen, in_sem.at[4])]
    for p in range(4):
        low = pl.multiple_of(ONE + rem(owner + 8 - p, 8) * SUB, 16)
        loads.append(pltpu.make_async_copy(
            win_hbm.at[pl.ds(low, SUB), :], cen_pair.at[pl.ds(p * SUB, SUB), :], in_sem.at[p]
        ))
    for load in loads:
        load.start()

    rows = rows_ref[...]
    offset = rows - me * 256
    mine = (offset >= 0) & (offset < 256)
    lanes = lax.broadcasted_iota(jnp.int32, (8, 128), 1)
    key = (lanes * 256 + offset).astype(jnp.float32)
    first, last = [], []
    for g in range(4):
        here = mine & (lanes >= g * 32) & (lanes < g * 32 + 32)
        first.append(jnp.min(jnp.where(here, key, 32767.0), axis=1, keepdims=True))
        last.append(jnp.max(jnp.where(here, key, 0.0), axis=1, keepdims=True))
    chosen = jnp.concatenate(first + last, axis=0).astype(jnp.int32)
    hot = jnp.bitwise_and(chosen, 255) == lax.broadcasted_iota(jnp.int32, (64, 256), 1)
    hot = hot.astype(jnp.float32).astype(jnp.bfloat16)
    buf_copy.wait()
    for q in range(8):
        piece = jnp.dot(
            hot, buf[:, q * 512:(q + 1) * 512], preferred_element_type=jnp.float32
        )
        for r in range(2):
            for g in range(4):
                stage[g, pl.ds(r * 8 + q, 32, stride=16), :] = (
                    piece[r * 32:r * 32 + 32, g * 128:(g + 1) * 128]
                )
    for g in range(4):
        send[:, g * 128:(g + 1) * 128] = stage[g].astype(jnp.bfloat16)

    pl.semaphore_wait(barrier, 36)

    def block_of(device):
        dc = rem(device, 2)
        dchip = device // 2
        dx, dy = dchip // 4, rem(dchip, 4)
        return dc * 16 + (dy + dc * (dx - dy)) * 4 + dx + dc * (dy - dx)

    def tile16(ref, index):
        return ref.at[pl.ds(pl.multiple_of(index * 16, 16), 16), :]

    def place(block):
        return rem(block, 4) * 8 + block // 4

    def push(k, carry):
        far = 32 - k
        tx, ty = rem(x + far // 8, 4), rem(y + rem(far, 8) // 2, 4)
        target = (tx * 4 + ty) * 2 + rem(core + far, 2)
        pltpu.make_async_remote_copy(
            src_ref=tile16(send, place(block_of(target))),
            dst_ref=tile16(recv, me),
            send_sem=a2a_send,
            recv_sem=a2a_recv,
            device_id={"buf": target},
            device_id_type=MESH,
        ).start()
        return carry

    lax.fori_loop(1, 32, push, 0)
    my_block = core * 16 + b * 4 + a
    own_copy = pltpu.make_async_copy(tile16(send, place(my_block)), tile16(recv, me), own_sem)
    own_copy.start()
    scale_copy = pltpu.make_async_remote_copy(
        src_ref=scale_ref, dst_ref=scale_pair, send_sem=z_send.at[0], recv_sem=z_recv.at[0],
        device_id={"lat": opposite}, device_id_type=MESH,
    )
    scale_copy.start()

    for load in loads:
        load.wait()

    def center(t, carry):
        at = pl.ds(pl.multiple_of(t * 32, 32), 32)
        cen[at, :] = (cen[at, :].astype(jnp.float32) - bias_ref[...]).astype(jnp.bfloat16)
        return carry

    def center_pair(t, carry):
        at = pl.ds(pl.multiple_of(t * 32, 32), 32)
        cen_pair[at, :] = (
            cen_pair[at, :].astype(jnp.float32) - bias_ref[...]
        ).astype(jnp.bfloat16)
        return carry

    lax.fori_loop(0, ONE // 32, center, 0)
    lax.fori_loop(0, 4 * SUB // 32, center_pair, 0)

    own_copy.wait()
    pltpu.make_async_copy(recv.at[pl.ds(0, 496), :], recv.at[pl.ds(0, 496), :], a2a_recv).wait()

    own = jnp.broadcast_to(rows_ref[pl.ds(my_block // 4, 1), :], (32, 128))
    own = lax.shift_right_logical(own, 8).astype(jnp.float32)
    entry = lax.broadcasted_iota(jnp.int32, (32, 128), 0)
    peer = lax.broadcasted_iota(jnp.int32, (32, 128), 1) - rem(my_block, 4) * 32
    source = jnp.sum(jnp.where(entry == peer, own, 0.0), axis=1, keepdims=True)
    twin = (own == source) & (peer >= 0) & (peer < entry)
    rank = jnp.sum(jnp.where(twin, 1.0, 0.0), axis=1, keepdims=True)
    code = (source * 16.0 + rank * 8.0).astype(jnp.int32)
    code = jnp.concatenate([code + q for q in range(8)], axis=0)
    hot = code == lax.broadcasted_iota(jnp.int32, (256, 512), 1)
    hot = hot.astype(jnp.float32).astype(jnp.bfloat16)
    picked[...] = jnp.dot(hot, recv[...], preferred_element_type=jnp.float32)
    squares = jnp.zeros((32, 512), jnp.float32)
    for q in range(8):
        value = picked[q * 32:q * 32 + 32, :]
        squares += value * value
    inverse = lax.rsqrt(jnp.sum(squares, axis=1, keepdims=True) + 1e-06)
    mine_at = pl.ds(pl.multiple_of(my_block * 32, 32), 32)
    for q in range(8):
        value = picked[q * 32:q * 32 + 32, :]
        units[0, mine_at, q * 512:q * 512 + 512] = (value * inverse).astype(jnp.bfloat16)

    def block_at(da, db):
        return core * 16 + rem(b + db + 4, 4) * 4 + rem(a + da + 4, 4)

    def device_at(da, db):
        pa, pb = rem(a + da + 4, 4), rem(b + db + 4, 4)
        px, py = pa + core * (pb - pa), pb + core * (pa - pb)
        return (px * 4 + py) * 2 + core

    sibling = me + 1 - 2 * core
    sent = [[], []]

    def block_ref(w, block, count=32, half=0):
        return units.at[w, pl.ds(pl.multiple_of(block * 32 + half * 16, 16), count), :]

    def give(w, block, target, count=32, half=0):
        at = block_ref(w, block, count, half)
        sem = ag_recv2 if half else ag_recv
        copy = pltpu.make_async_remote_copy(
            src_ref=at, dst_ref=at, send_sem=ag_send.at[w, len(sent[w])],
            recv_sem=sem.at[w, block], device_id={"buf": target}, device_id_type=MESH,
        )
        copy.start()
        sent[w].append(copy)

    def arrive(w, block, count=32, half=0):
        at = block_ref(w, block, count, half)
        sem = ag_recv2 if half else ag_recv
        pltpu.make_async_copy(at, at, sem.at[w, block]).wait()

    def spread(w, block):
        give(w, block, device_at(0, 1))
        give(w, block, device_at(0, -1))
        give(w, block, sibling)

    def second(w, da):
        block = block_at(da, -1)
        arrive(w, block)
        give(w, block, device_at(0, 1), 16, 0)
        give(w, block, sibling)
        block = block_at(da, 1)
        arrive(w, block)
        give(w, block, device_at(0, -1), 16, 1)
        give(w, block, sibling)

    def far(w, da):
        block = block_at(da, 2)
        arrive(w, block, 16, 0)
        arrive(w, block, 16, 1)
        give(w, block, sibling)

    def step(w, n):
        if n == 0:
            give(w, my_block, device_at(1, 0))
            give(w, my_block, device_at(-1, 0))
            spread(w, my_block)
        elif n == 1:
            block = block_at(-1, 0)
            arrive(w, block)
            give(w, block, device_at(1, 0), 16, 0)
            spread(w, block)
        elif n == 2:
            block = block_at(1, 0)
            arrive(w, block)
            give(w, block, device_at(-1, 0), 16, 1)
            spread(w, block)
        elif n == 3:
            second(w, 0)
        elif n == 4:
            block = block_at(2, 0)
            arrive(w, block, 16, 0)
            arrive(w, block, 16, 1)
            spread(w, block)
        elif n < 8:
            second(w, (-1, 1, 2)[n - 5])
        else:
            far(w, (0, -1, 1, 2)[n - 8])

    step(0, 0)
    z_copy = pltpu.make_async_remote_copy(
        src_ref=block_ref(0, my_block), dst_ref=block_ref(1, my_block),
        send_sem=z_send.at[1], recv_sem=z_recv.at[1],
        device_id={"lat": opposite}, device_id_type=MESH,
    )
    z_copy.start()
    for n in range(1, 8):
        step(0, n)

    def encode(group):
        at = pl.ds(pl.multiple_of(group * 256, 256), 256)
        scores = lax.dot_general(
            cen[...], units[0, at, :], NT, preferred_element_type=jnp.float32
        )
        act[:, at] = jnp.maximum(scores * scale_ref[:, at], 0.0).astype(jnp.bfloat16)

    def encode_pair(w, group):
        at = pl.ds(pl.multiple_of(group * 256, 256), 256)
        scale = (scale_pair if w else scale_ref)[:, at]
        scores = lax.dot_general(
            cen_pair[...], units[w, at, :], NT, preferred_element_type=jnp.float32
        )
        act_pair[w, :, at] = jnp.maximum(scores * scale, 0.0).astype(jnp.bfloat16)

    other = 1 - core
    other_b = x + core * (y - x)
    mine_near = core * 2 + b // 2
    mine_far = core * 2 + 1 - b // 2
    other_near = other * 2 + other_b // 2
    other_far = other * 2 + 1 - other_b // 2

    def arrive_group(w, group):
        def one(i, carry):
            arrive(w, group * 8 + i)
            return carry

        lax.fori_loop(0, 8, one, 0)

    encode(mine_near)
    for n in range(8, 12):
        step(0, n)
    z_copy.wait_recv()
    step(1, 0)
    arrive_group(0, other_near)
    encode(other_near)
    encode(mine_far)
    arrive_group(0, other_far)
    encode(other_far)

    def decode(target):
        columns = pl.ds(pl.multiple_of(target * 512, 512), 512)
        value = jnp.dot(act[...], units[0, :, columns], preferred_element_type=jnp.float32)
        part[target] = value.astype(jnp.bfloat16)

    def half_of(ref, half):
        return ref.at[pl.ds(half * HALF, HALF), :]

    def rs_copy(i, source, flow, way):
        return pltpu.make_async_remote_copy(
            src_ref=source, dst_ref=flow.at[i],
            send_sem=rs_send.at[way, i], recv_sem=rs_recv.at[way, i],
            device_id={"lat": left if way else right}, device_id_type=MESH,
        )

    def rs_wait(i, flow, way):
        pltpu.make_async_copy(flow.at[i], flow.at[i], rs_recv.at[way, i]).wait()

    def hop(i):
        for way, flow in ((0, flow_r), (1, flow_l)):
            low = ((i + way) % 2) * HALF
            away = 4 - (i + 1) // 2
            target = rem(owner + (8 - away if way else away), 8)
            rs_wait(i - 2, flow, way)
            total = flow[i - 2].astype(jnp.float32)
            total += part[target, low:low + HALF, :].astype(jnp.float32)
            flow[i - 2] = total.astype(jnp.bfloat16)
            rs_copy(i, flow.at[i - 2], flow, way).start()

    decode(opposite)
    rs_copy(0, half_of(part.at[opposite], 0), flow_r, 0).start()
    rs_copy(0, half_of(part.at[opposite], 1), flow_l, 1).start()

    def decode_next(i, carry):
        decode(rem(owner + 3 + 2 * i, 8))
        return carry

    lax.fori_loop(0, 2, decode_next, 0)
    rs_copy(1, half_of(part.at[rem(owner + 3, 8)], 1), flow_r, 0).start()
    rs_copy(1, half_of(part.at[rem(owner + 5, 8)], 0), flow_l, 1).start()
    step(1, 1)
    step(1, 2)

    def decode_rest(i, carry):
        decode(rem(owner + 6 + i, 8))
        return carry

    lax.fori_loop(0, 5, decode_rest, 0)
    step(1, 3)
    hop(2)
    step(1, 4)
    lax.fori_loop(0, 4, lambda i, carry: (encode_pair(0, i), carry)[1], 0)
    step(1, 5)
    hop(3)
    step(1, 6)
    scale_copy.wait_recv()
    hop(4)
    step(1, 7)
    encode_pair(1, mine_near)
    hop(5)
    for n in range(8, 12):
        step(1, n)
    arrive_group(1, other_near)
    encode_pair(1, other_near)
    encode_pair(1, mine_far)
    arrive_group(1, other_far)
    encode_pair(1, other_far)
    hop(6)

    def decode_pair(o, carry):
        columns = pl.ds(pl.multiple_of(rem(owner + o, 8) * 512, 512), 512)
        value = jnp.dot(act_pair[0], units[0, :, columns], preferred_element_type=jnp.float32)
        value += jnp.dot(act_pair[1], units[1, :, columns], preferred_element_type=jnp.float32)
        value = value.astype(jnp.bfloat16)
        for p in range(4):
            for c in range(PIECES):
                low = p * SUB + c * 16
                part_pair[c, p, o] = value[low:low + 16, :]
        return carry

    pair_copies = []

    def pair_give(way, c, p, source, dest, distance=1, slot=None):
        slot = p if slot is None else slot
        copy = pltpu.make_async_remote_copy(
            src_ref=source, dst_ref=dest,
            send_sem=pair_send.at[way, c, slot], recv_sem=pair_recv.at[way, c, slot],
            device_id={"lat": rem(owner + (8 - distance if way else distance), 8)},
            device_id_type=MESH,
        )
        copy.start()
        pair_copies.append(copy)

    def pair_wait(way, c, p):
        if p == 4:
            at = pair_far.at[way, c]
        else:
            at = pair_flow.at[way, c, p, pl.ds(0, 5 - p if p < 3 else 1)]
        pltpu.make_async_copy(at, at, pair_recv.at[way, c, p]).wait()

    lax.fori_loop(1, 8, decode_pair, 0)
    for c in range(PIECES):
        for way in range(2):
            source = part_pair.at[c, 3 if way else 0, pl.ds(3 if way else 1, 5)]
            pair_give(way, c, 0, source, pair_flow.at[way, c, 0])
    decode_pair(0, 0)

    bias = bias_ref[:, pl.ds(pl.multiple_of(owner * 512, 512), 512)]

    def finish_one():
        for i in (5, 6):
            rs_wait(i, flow_r, 0)
            rs_wait(i, flow_l, 1)
        for half in range(2):
            at = slice(half * HALF, half * HALF + HALF)
            total = part[owner, at, :].astype(jnp.float32) + bias
            total += flow_r[6 - half].astype(jnp.float32) + flow_l[5 + half].astype(jnp.float32)
            out_ref[at, :] = total.astype(jnp.bfloat16)

    for p in range(1, 4):
        for c in range(PIECES):
            for way in range(2):
                pair_wait(way, c, p - 1)
                low = 0 if way else 1
                for k in range(5 - p):
                    mine_part = part_pair[c, 3 - p, 3 + p + k] if way else part_pair[c, p, 1 + k]
                    total = pair_flow[way, c, p - 1, low + k].astype(jnp.float32)
                    total += mine_part.astype(jnp.float32)
                    pair_flow[way, c, p - 1, low + k] = total.astype(jnp.bfloat16)
                source = pair_flow.at[way, c, p - 1, pl.ds(low, 5 - p)]
                if p < 3:
                    pair_give(way, c, p, source, pair_flow.at[way, c, p, pl.ds(0, 5 - p)])
                else:
                    pair_give(way, c, 4, source.at[0 if way else 1], pair_far.at[way, c], 2, 4)
                    pair_give(way, c, 3, source.at[1 if way else 0], pair_flow.at[way, c, 3, 0])
        if p == 1:
            finish_one()
    for c in range(PIECES):
        for way in range(2):
            pair_wait(way, c, 3)
            pair_wait(way, c, 4)

    for c in range(PIECES):
        for r in range(-4, 4):
            terms = []
            if -3 <= r <= 0:
                terms.append(part_pair[c, -r, 0])
            for p in range(4):
                if (r + 1 + p) % 8 == 0:
                    terms.append(pair_flow[0, c, p, 0])
                if (r + 2 - p) % 8 == 0:
                    terms.append(pair_flow[1, c, p, 4 - p if p < 3 else 0])
            if r == 3:
                terms.append(pair_far[0, c])
            if r == 2:
                terms.append(pair_far[1, c])
            total = jnp.broadcast_to(bias, (16, 512))
            for term in terms:
                total += term.astype(jnp.float32)
            low = pl.multiple_of(ONE + rem(owner + 8 + r, 8) * SUB + c * 16, 16)
            out_ref[pl.ds(low, 16), :] = total.astype(jnp.bfloat16)

    pltpu.make_async_copy(send.at[pl.ds(0, 496), :], send.at[pl.ds(0, 496), :], a2a_send).wait()
    for copy in [scale_copy, z_copy] + sent[0] + sent[1] + pair_copies:
        copy.wait_send()

    def drain(i, carry):
        for way in range(2):
            pltpu.make_async_copy(flow_r.at[i], flow_r.at[i], rs_send.at[way, i]).wait()
        return carry

    lax.fori_loop(0, 7, drain, 0)


def on_device(buffer, sample_rows, window, enc_scale, dec_bias):
    vmem = pl.BlockSpec(memory_space=pltpu.VMEM)
    anywhere = pl.BlockSpec(memory_space=pl.ANY)
    call = pl.pallas_call(
        fused,
        out_shape=jax.ShapeDtypeStruct((768, 512), jnp.bfloat16),
        in_specs=[vmem, anywhere, anywhere, vmem, vmem],
        out_specs=vmem,
        scratch_shapes=[
            pltpu.VMEM((256, 4096), jnp.bfloat16),
            pltpu.VMEM((4, 512, 128), jnp.float32),
            pltpu.VMEM((512, 512), jnp.bfloat16),
            pltpu.VMEM((512, 512), jnp.bfloat16),
            pltpu.VMEM((256, 512), jnp.float32),
            pltpu.VMEM((2, 1024, 4096), jnp.bfloat16),
            pltpu.VMEM((ONE, 4096), jnp.bfloat16),
            pltpu.VMEM((4 * SUB, 4096), jnp.bfloat16),
            pltpu.VMEM((ONE, 1024), jnp.bfloat16),
            pltpu.VMEM((2, 4 * SUB, 1024), jnp.bfloat16),
            pltpu.VMEM((8, ONE, 512), jnp.bfloat16),
            pltpu.VMEM((7, HALF, 512), jnp.bfloat16),
            pltpu.VMEM((7, HALF, 512), jnp.bfloat16),
            pltpu.VMEM((PIECES, 4, 8, 16, 512), jnp.bfloat16),
            pltpu.VMEM((2, PIECES, 4, 5, 16, 512), jnp.bfloat16),
            pltpu.VMEM((2, PIECES, 16, 512), jnp.bfloat16),
            pltpu.VMEM((1, 1024), jnp.float32),
            pltpu.SemaphoreType.DMA((5,)),
            pltpu.SemaphoreType.DMA,
            pltpu.SemaphoreType.DMA,
            pltpu.SemaphoreType.DMA,
            pltpu.SemaphoreType.DMA((2,)),
            pltpu.SemaphoreType.DMA((2,)),
            pltpu.SemaphoreType.DMA((2, 40)),
            pltpu.SemaphoreType.DMA((2, 32)),
            pltpu.SemaphoreType.DMA((2, 32)),
            pltpu.SemaphoreType.DMA((2, 7)),
            pltpu.SemaphoreType.DMA((2, 7)),
            pltpu.SemaphoreType.DMA((2, PIECES, 5)),
            pltpu.SemaphoreType.DMA((2, PIECES, 5)),
        ],
        compiler_params=pltpu.CompilerParams(
            collective_id=0, has_side_effects=True, vmem_limit_bytes=56 * 1024 * 1024
        ),
    )
    return call(
        sample_rows.reshape(8, 128), buffer, window,
        enc_scale.reshape(1, 1024), dec_bias.reshape(1, 4096),
    )


def solution(mesh):
    in_specs = (P("buf", None), P("lat"), P("buf", None), P("lat"), P())
    out_specs = P("buf", "lat")
    return jax.shard_map(
        on_device, mesh=mesh, in_specs=in_specs, out_specs=out_specs, check_vma=False
    )
```

```python
import jax
import jax.numpy as jnp
from jax import lax
from jax.experimental import pallas as pl
from jax.experimental.pallas import tpu as pltpu
from jax.sharding import PartitionSpec as P

MESH = pl.DeviceIdType.MESH
NT = (((1,), (1,)), ((), ()))
ONE = 384
HALF = ONE // 2
PIECES = 3
SUB = 16 * PIECES


def rem(value, size):
    return lax.rem(value, size)


def fused(
    rows_ref, buf_hbm, win_hbm, scale_ref, bias_ref, out_hbm,
    out_ref,    buf, stage, send, recv, picked, units, cen, cen_pair, act, act_pair,
    part, flow_r, flow_l, part_pair, pair_flow, pair_far, scale_pair,
    in_sem, own_sem, a2a_send, a2a_recv, z_send, z_recv, ag_send, ag_recv, ag_recv2,
    rs_send, rs_recv, pair_send, pair_recv,
):
    me = lax.axis_index("buf")
    owner = lax.axis_index("lat")
    core = rem(me, 2)
    chip = me // 2
    x, y = chip // 4, rem(chip, 4)
    a = x + core * (y - x)
    b = y + core * (x - y)
    right, left, opposite = rem(owner + 1, 8), rem(owner + 7, 8), rem(owner + 4, 8)

    barrier = pltpu.get_barrier_semaphore()

    def greet(k, carry):
        pl.semaphore_signal(
            barrier, inc=1, device_id={"buf": rem(me + k, 32)}, device_id_type=MESH
        )
        return carry

    lax.fori_loop(1, 32, greet, 0)
    for k in (1, 2, 4, 6, 7):
        pl.semaphore_signal(barrier, inc=1, device_id={"lat": rem(owner + k, 8)}, device_id_type=MESH)

    buf_copy = pltpu.make_async_copy(buf_hbm, buf, own_sem)
    buf_copy.start()
    loads = [pltpu.make_async_copy(win_hbm.at[pl.ds(0, ONE), :], cen, in_sem.at[4])]
    for p in range(4):
        low = pl.multiple_of(ONE + rem(owner + 8 - p, 8) * SUB, 16)
        loads.append(pltpu.make_async_copy(
            win_hbm.at[pl.ds(low, SUB), :], cen_pair.at[pl.ds(p * SUB, SUB), :], in_sem.at[p]
        ))
    for load in loads:
        load.start()

    rows = rows_ref[...]
    offset = rows - me * 256
    mine = (offset >= 0) & (offset < 256)
    lanes = lax.broadcasted_iota(jnp.int32, (8, 128), 1)
    key = (lanes * 256 + offset).astype(jnp.float32)
    first, last = [], []
    for g in range(4):
        here = mine & (lanes >= g * 32) & (lanes < g * 32 + 32)
        first.append(jnp.min(jnp.where(here, key, 32767.0), axis=1, keepdims=True))
        last.append(jnp.max(jnp.where(here, key, 0.0), axis=1, keepdims=True))
    chosen = jnp.concatenate(first + last, axis=0).astype(jnp.int32)
    hot = jnp.bitwise_and(chosen, 255) == lax.broadcasted_iota(jnp.int32, (64, 256), 1)
    hot = hot.astype(jnp.float32).astype(jnp.bfloat16)
    buf_copy.wait()
    for q in range(8):
        piece = jnp.dot(
            hot, buf[:, q * 512:(q + 1) * 512], preferred_element_type=jnp.float32
        )
        for r in range(2):
            for g in range(4):
                stage[g, pl.ds(r * 8 + q, 32, stride=16), :] = (
                    piece[r * 32:r * 32 + 32, g * 128:(g + 1) * 128]
                )
    for g in range(4):
        send[:, g * 128:(g + 1) * 128] = stage[g].astype(jnp.bfloat16)

    pl.semaphore_wait(barrier, 36)

    def block_of(device):
        dc = rem(device, 2)
        dchip = device // 2
        dx, dy = dchip // 4, rem(dchip, 4)
        return dc * 16 + (dy + dc * (dx - dy)) * 4 + dx + dc * (dy - dx)

    def tile16(ref, index):
        return ref.at[pl.ds(pl.multiple_of(index * 16, 16), 16), :]

    def place(block):
        return rem(block, 4) * 8 + block // 4

    def push(k, carry):
        far = 32 - k
        tx, ty = rem(x + far // 8, 4), rem(y + rem(far, 8) // 2, 4)
        target = (tx * 4 + ty) * 2 + rem(core + far, 2)
        pltpu.make_async_remote_copy(
            src_ref=tile16(send, place(block_of(target))),
            dst_ref=tile16(recv, me),
            send_sem=a2a_send,
            recv_sem=a2a_recv,
            device_id={"buf": target},
            device_id_type=MESH,
        ).start()
        return carry

    lax.fori_loop(1, 32, push, 0)
    my_block = core * 16 + b * 4 + a
    own_copy = pltpu.make_async_copy(tile16(send, place(my_block)), tile16(recv, me), own_sem)
    own_copy.start()
    scale_copy = pltpu.make_async_remote_copy(
        src_ref=scale_ref, dst_ref=scale_pair, send_sem=z_send.at[0], recv_sem=z_recv.at[0],
        device_id={"lat": opposite}, device_id_type=MESH,
    )
    scale_copy.start()

    for load in loads:
        load.wait()

    def center(t, carry):
        at = pl.ds(pl.multiple_of(t * 32, 32), 32)
        cen[at, :] = (cen[at, :].astype(jnp.float32) - bias_ref[...]).astype(jnp.bfloat16)
        return carry

    def center_pair(t, carry):
        at = pl.ds(pl.multiple_of(t * 32, 32), 32)
        cen_pair[at, :] = (
            cen_pair[at, :].astype(jnp.float32) - bias_ref[...]
        ).astype(jnp.bfloat16)
        return carry

    lax.fori_loop(0, ONE // 32, center, 0)
    lax.fori_loop(0, 4 * SUB // 32, center_pair, 0)

    own_copy.wait()
    pltpu.make_async_copy(recv.at[pl.ds(0, 496), :], recv.at[pl.ds(0, 496), :], a2a_recv).wait()

    own = jnp.broadcast_to(rows_ref[pl.ds(my_block // 4, 1), :], (32, 128))
    own = lax.shift_right_logical(own, 8).astype(jnp.float32)
    entry = lax.broadcasted_iota(jnp.int32, (32, 128), 0)
    peer = lax.broadcasted_iota(jnp.int32, (32, 128), 1) - rem(my_block, 4) * 32
    source = jnp.sum(jnp.where(entry == peer, own, 0.0), axis=1, keepdims=True)
    twin = (own == source) & (peer >= 0) & (peer < entry)
    rank = jnp.sum(jnp.where(twin, 1.0, 0.0), axis=1, keepdims=True)
    code = (source * 16.0 + rank * 8.0).astype(jnp.int32)
    code = jnp.concatenate([code + q for q in range(8)], axis=0)
    hot = code == lax.broadcasted_iota(jnp.int32, (256, 512), 1)
    hot = hot.astype(jnp.float32).astype(jnp.bfloat16)
    picked[...] = jnp.dot(hot, recv[...], preferred_element_type=jnp.float32)
    squares = jnp.zeros((32, 512), jnp.float32)
    for q in range(8):
        value = picked[q * 32:q * 32 + 32, :]
        squares += value * value
    inverse = lax.rsqrt(jnp.sum(squares, axis=1, keepdims=True) + 1e-06)
    mine_at = pl.ds(pl.multiple_of(my_block * 32, 32), 32)
    for q in range(8):
        value = picked[q * 32:q * 32 + 32, :]
        units[0, mine_at, q * 512:q * 512 + 512] = (value * inverse).astype(jnp.bfloat16)

    def block_at(da, db):
        return core * 16 + rem(b + db + 4, 4) * 4 + rem(a + da + 4, 4)

    def device_at(da, db):
        pa, pb = rem(a + da + 4, 4), rem(b + db + 4, 4)
        px, py = pa + core * (pb - pa), pb + core * (pa - pb)
        return (px * 4 + py) * 2 + core

    sibling = me + 1 - 2 * core
    sent = [[], []]

    def block_ref(w, block, count=32, half=0):
        return units.at[w, pl.ds(pl.multiple_of(block * 32 + half * 16, 16), count), :]

    def give(w, block, target, count=32, half=0):
        at = block_ref(w, block, count, half)
        sem = ag_recv2 if half else ag_recv
        copy = pltpu.make_async_remote_copy(
            src_ref=at, dst_ref=at, send_sem=ag_send.at[w, len(sent[w])],
            recv_sem=sem.at[w, block], device_id={"buf": target}, device_id_type=MESH,
        )
        copy.start()
        sent[w].append(copy)

    def arrive(w, block, count=32, half=0):
        at = block_ref(w, block, count, half)
        sem = ag_recv2 if half else ag_recv
        pltpu.make_async_copy(at, at, sem.at[w, block]).wait()

    def spread(w, block):
        give(w, block, device_at(0, 1))
        give(w, block, device_at(0, -1))
        give(w, block, sibling)

    def second(w, da):
        block = block_at(da, -1)
        arrive(w, block)
        give(w, block, device_at(0, 1), 16, 0)
        give(w, block, sibling)
        block = block_at(da, 1)
        arrive(w, block)
        give(w, block, device_at(0, -1), 16, 1)
        give(w, block, sibling)

    def far(w, da):
        block = block_at(da, 2)
        arrive(w, block, 16, 0)
        arrive(w, block, 16, 1)
        give(w, block, sibling)

    def step(w, n):
        if n == 0:
            give(w, my_block, device_at(1, 0))
            give(w, my_block, device_at(-1, 0))
            spread(w, my_block)
        elif n == 1:
            block = block_at(-1, 0)
            arrive(w, block)
            give(w, block, device_at(1, 0), 16, 0)
            spread(w, block)
        elif n == 2:
            block = block_at(1, 0)
            arrive(w, block)
            give(w, block, device_at(-1, 0), 16, 1)
            spread(w, block)
        elif n == 3:
            second(w, 0)
        elif n == 4:
            block = block_at(2, 0)
            arrive(w, block, 16, 0)
            arrive(w, block, 16, 1)
            spread(w, block)
        elif n < 8:
            second(w, (-1, 1, 2)[n - 5])
        else:
            far(w, (0, -1, 1, 2)[n - 8])

    step(0, 0)
    z_copy = pltpu.make_async_remote_copy(
        src_ref=block_ref(0, my_block), dst_ref=block_ref(1, my_block),
        send_sem=z_send.at[1], recv_sem=z_recv.at[1],
        device_id={"lat": opposite}, device_id_type=MESH,
    )
    z_copy.start()
    for n in range(1, 8):
        step(0, n)

    def encode(group):
        at = pl.ds(pl.multiple_of(group * 256, 256), 256)
        scores = lax.dot_general(
            cen[...], units[0, at, :], NT, preferred_element_type=jnp.float32
        )
        act[:, at] = jnp.maximum(scores * scale_ref[:, at], 0.0).astype(jnp.bfloat16)

    def encode_pair(w, group):
        at = pl.ds(pl.multiple_of(group * 256, 256), 256)
        scale = (scale_pair if w else scale_ref)[:, at]
        scores = lax.dot_general(
            cen_pair[...], units[w, at, :], NT, preferred_element_type=jnp.float32
        )
        act_pair[w, :, at] = jnp.maximum(scores * scale, 0.0).astype(jnp.bfloat16)

    other = 1 - core
    other_b = x + core * (y - x)
    mine_near = core * 2 + b // 2
    mine_far = core * 2 + 1 - b // 2
    other_near = other * 2 + other_b // 2
    other_far = other * 2 + 1 - other_b // 2

    def arrive_group(w, group):
        def one(i, carry):
            arrive(w, group * 8 + i)
            return carry

        lax.fori_loop(0, 8, one, 0)

    encode(mine_near)
    arrive_group(0, other_near)
    encode(other_near)
    for n in range(8, 12):
        step(0, n)
    z_copy.wait_recv()
    step(1, 0)
    encode(mine_far)
    arrive_group(0, other_far)
    encode(other_far)

    def decode(target):
        columns = pl.ds(pl.multiple_of(target * 512, 512), 512)
        value = jnp.dot(act[...], units[0, :, columns], preferred_element_type=jnp.float32)
        part[target] = value.astype(jnp.bfloat16)

    def half_of(ref, half):
        return ref.at[pl.ds(half * HALF, HALF), :]

    def rs_copy(i, source, flow, way):
        return pltpu.make_async_remote_copy(
            src_ref=source, dst_ref=flow.at[i],
            send_sem=rs_send.at[way, i], recv_sem=rs_recv.at[way, i],
            device_id={"lat": left if way else right}, device_id_type=MESH,
        )

    def rs_wait(i, flow, way):
        pltpu.make_async_copy(flow.at[i], flow.at[i], rs_recv.at[way, i]).wait()

    def hop(i):
        for way, flow in ((0, flow_r), (1, flow_l)):
            low = ((i + way) % 2) * HALF
            away = 4 - (i + 1) // 2
            target = rem(owner + (8 - away if way else away), 8)
            rs_wait(i - 2, flow, way)
            total = flow[i - 2].astype(jnp.float32)
            total += part[target, low:low + HALF, :].astype(jnp.float32)
            flow[i - 2] = total.astype(jnp.bfloat16)
            rs_copy(i, flow.at[i - 2], flow, way).start()

    decode(opposite)
    rs_copy(0, half_of(part.at[opposite], 0), flow_r, 0).start()
    rs_copy(0, half_of(part.at[opposite], 1), flow_l, 1).start()

    def decode_next(i, carry):
        decode(rem(owner + 3 + 2 * i, 8))
        return carry

    lax.fori_loop(0, 2, decode_next, 0)
    rs_copy(1, half_of(part.at[rem(owner + 3, 8)], 1), flow_r, 0).start()
    rs_copy(1, half_of(part.at[rem(owner + 5, 8)], 0), flow_l, 1).start()
    step(1, 1)
    step(1, 2)

    def decode_rest(i, carry):
        decode(rem(owner + 6 + i, 8))
        return carry

    lax.fori_loop(0, 5, decode_rest, 0)
    step(1, 3)
    hop(2)
    step(1, 4)
    lax.fori_loop(0, 4, lambda i, carry: (encode_pair(0, i), carry)[1], 0)
    step(1, 5)
    hop(3)
    step(1, 6)
    scale_copy.wait_recv()
    hop(4)
    step(1, 7)
    encode_pair(1, mine_near)
    hop(5)
    for n in range(8, 12):
        step(1, n)
    arrive_group(1, other_near)
    encode_pair(1, other_near)
    encode_pair(1, mine_far)
    arrive_group(1, other_far)
    encode_pair(1, other_far)
    hop(6)

    def decode_pair(o, carry):
        columns = pl.ds(pl.multiple_of(rem(owner + o, 8) * 512, 512), 512)
        value = jnp.dot(act_pair[0], units[0, :, columns], preferred_element_type=jnp.float32)
        value += jnp.dot(act_pair[1], units[1, :, columns], preferred_element_type=jnp.float32)
        value = value.astype(jnp.bfloat16)
        for p in range(4):
            for c in range(PIECES):
                low = p * SUB + c * 16
                part_pair[c, p, o] = value[low:low + 16, :]
        return carry

    pair_copies = []

    def pair_give(way, c, p, source, dest, distance=1, slot=None):
        slot = p if slot is None else slot
        copy = pltpu.make_async_remote_copy(
            src_ref=source, dst_ref=dest,
            send_sem=pair_send.at[way, c, slot], recv_sem=pair_recv.at[way, c, slot],
            device_id={"lat": rem(owner + (8 - distance if way else distance), 8)},
            device_id_type=MESH,
        )
        copy.start()
        pair_copies.append(copy)

    def pair_wait(way, c, p):
        if p == 4:
            at = pair_far.at[way, c]
        else:
            at = pair_flow.at[way, c, p, pl.ds(0, 5 - p if p < 3 else 1)]
        pltpu.make_async_copy(at, at, pair_recv.at[way, c, p]).wait()

    lax.fori_loop(1, 8, decode_pair, 0)
    for c in range(PIECES):
        for way in range(2):
            source = part_pair.at[c, 3 if way else 0, pl.ds(3 if way else 1, 5)]
            pair_give(way, c, 0, source, pair_flow.at[way, c, 0])
    decode_pair(0, 0)

    bias = bias_ref[:, pl.ds(pl.multiple_of(owner * 512, 512), 512)]

    def out_copy(n):
        at = pl.ds(ONE, 768 - ONE) if n else pl.ds(0, ONE)
        return pltpu.make_async_copy(out_ref.at[at, :], out_hbm.at[at, :], in_sem.at[n])

    def finish_one():
        for i in (5, 6):
            rs_wait(i, flow_r, 0)
            rs_wait(i, flow_l, 1)
        for half in range(2):
            at = slice(half * HALF, half * HALF + HALF)
            total = part[owner, at, :].astype(jnp.float32) + bias
            total += flow_r[6 - half].astype(jnp.float32) + flow_l[5 + half].astype(jnp.float32)
            out_ref[at, :] = total.astype(jnp.bfloat16)
        out_copy(0).start()

    for p in range(1, 4):
        for c in range(PIECES):
            for way in range(2):
                pair_wait(way, c, p - 1)
                low = 0 if way else 1
                for k in range(5 - p):
                    mine_part = part_pair[c, 3 - p, 3 + p + k] if way else part_pair[c, p, 1 + k]
                    total = pair_flow[way, c, p - 1, low + k].astype(jnp.float32)
                    total += mine_part.astype(jnp.float32)
                    pair_flow[way, c, p - 1, low + k] = total.astype(jnp.bfloat16)
                source = pair_flow.at[way, c, p - 1, pl.ds(low, 5 - p)]
                if p < 3:
                    pair_give(way, c, p, source, pair_flow.at[way, c, p, pl.ds(0, 5 - p)])
                else:
                    pair_give(way, c, 4, source.at[0 if way else 1], pair_far.at[way, c], 2, 4)
                    pair_give(way, c, 3, source.at[1 if way else 0], pair_flow.at[way, c, 3, 0])
        if p == 1:
            finish_one()
    for c in range(PIECES):
        for way in range(2):
            pair_wait(way, c, 3)
            pair_wait(way, c, 4)

    for c in range(PIECES):
        for r in range(-4, 4):
            terms = []
            if -3 <= r <= 0:
                terms.append(part_pair[c, -r, 0])
            for p in range(4):
                if (r + 1 + p) % 8 == 0:
                    terms.append(pair_flow[0, c, p, 0])
                if (r + 2 - p) % 8 == 0:
                    terms.append(pair_flow[1, c, p, 4 - p if p < 3 else 0])
            if r == 3:
                terms.append(pair_far[0, c])
            if r == 2:
                terms.append(pair_far[1, c])
            total = jnp.broadcast_to(bias, (16, 512))
            for term in terms:
                total += term.astype(jnp.float32)
            low = pl.multiple_of(ONE + rem(owner + 8 + r, 8) * SUB + c * 16, 16)
            out_ref[pl.ds(low, 16), :] = total.astype(jnp.bfloat16)

    out_copy(1).start()

    pltpu.make_async_copy(send.at[pl.ds(0, 496), :], send.at[pl.ds(0, 496), :], a2a_send).wait()
    for copy in [scale_copy, z_copy] + sent[0] + sent[1] + pair_copies:
        copy.wait_send()

    def drain(i, carry):
        for way in range(2):
            pltpu.make_async_copy(flow_r.at[i], flow_r.at[i], rs_send.at[way, i]).wait()
        return carry

    lax.fori_loop(0, 7, drain, 0)
    out_copy(0).wait()
    out_copy(1).wait()


def on_device(buffer, sample_rows, window, enc_scale, dec_bias):
    vmem = pl.BlockSpec(memory_space=pltpu.VMEM)
    anywhere = pl.BlockSpec(memory_space=pl.ANY)
    call = pl.pallas_call(
        fused,
        out_shape=jax.ShapeDtypeStruct((768, 512), jnp.bfloat16),
        in_specs=[vmem, anywhere, anywhere, vmem, vmem],
        out_specs=anywhere,
        scratch_shapes=[
            pltpu.VMEM((768, 512), jnp.bfloat16),
            pltpu.VMEM((256, 4096), jnp.bfloat16),
            pltpu.VMEM((4, 512, 128), jnp.float32),
            pltpu.VMEM((512, 512), jnp.bfloat16),
            pltpu.VMEM((512, 512), jnp.bfloat16),
            pltpu.VMEM((256, 512), jnp.float32),
            pltpu.VMEM((2, 1024, 4096), jnp.bfloat16),
            pltpu.VMEM((ONE, 4096), jnp.bfloat16),
            pltpu.VMEM((4 * SUB, 4096), jnp.bfloat16),
            pltpu.VMEM((ONE, 1024), jnp.bfloat16),
            pltpu.VMEM((2, 4 * SUB, 1024), jnp.bfloat16),
            pltpu.VMEM((8, ONE, 512), jnp.bfloat16),
            pltpu.VMEM((7, HALF, 512), jnp.bfloat16),
            pltpu.VMEM((7, HALF, 512), jnp.bfloat16),
            pltpu.VMEM((PIECES, 4, 8, 16, 512), jnp.bfloat16),
            pltpu.VMEM((2, PIECES, 4, 5, 16, 512), jnp.bfloat16),
            pltpu.VMEM((2, PIECES, 16, 512), jnp.bfloat16),
            pltpu.VMEM((1, 1024), jnp.float32),
            pltpu.SemaphoreType.DMA((5,)),
            pltpu.SemaphoreType.DMA,
            pltpu.SemaphoreType.DMA,
            pltpu.SemaphoreType.DMA,
            pltpu.SemaphoreType.DMA((2,)),
            pltpu.SemaphoreType.DMA((2,)),
            pltpu.SemaphoreType.DMA((2, 40)),
            pltpu.SemaphoreType.DMA((2, 32)),
            pltpu.SemaphoreType.DMA((2, 32)),
            pltpu.SemaphoreType.DMA((2, 7)),
            pltpu.SemaphoreType.DMA((2, 7)),
            pltpu.SemaphoreType.DMA((2, PIECES, 5)),
            pltpu.SemaphoreType.DMA((2, PIECES, 5)),
        ],
        compiler_params=pltpu.CompilerParams(
            collective_id=0, has_side_effects=True, vmem_limit_bytes=52 * 1024 * 1024
        ),
    )
    return call(
        sample_rows.reshape(8, 128), buffer, window,
        enc_scale.reshape(1, 1024), dec_bias.reshape(1, 4096),
    )


def solution(mesh):
    in_specs = (P("buf", None), P("lat"), P("buf", None), P("lat"), P())
    out_specs = P("buf", "lat")
    return jax.shard_map(
        on_device, mesh=mesh, in_specs=in_specs, out_specs=out_specs, check_vma=False
    )
```

```python
import jax
import jax.numpy as jnp
from jax import lax
from jax.experimental import pallas as pl
from jax.experimental.pallas import tpu as pltpu
from jax.sharding import PartitionSpec as P

MESH = pl.DeviceIdType.MESH
NT = (((1,), (1,)), ((), ()))
ONE = 384
HALF = ONE // 2
PIECES = 3
SUB = 16 * PIECES


def rem(value, size):
    return lax.rem(value, size)


def fused(
    rows_ref, buf_hbm, win_hbm, scale_ref, bias_ref, out_hbm,
    out_ref,    buf, stage, send, recv, picked, units, cen, cen_pair, act, act_pair,
    part, flow_r, flow_l, part_pair, pair_flow, pair_far, scale_pair,
    in_sem, own_sem, a2a_send, a2a_recv, z_send, z_recv, ag_send, ag_recv, ag_recv2,
    rs_send, rs_recv, pair_send, pair_recv,
):
    me = lax.axis_index("buf")
    owner = lax.axis_index("lat")
    core = rem(me, 2)
    chip = me // 2
    x, y = chip // 4, rem(chip, 4)
    a = x + core * (y - x)
    b = y + core * (x - y)
    right, left, opposite = rem(owner + 1, 8), rem(owner + 7, 8), rem(owner + 4, 8)

    barrier = pltpu.get_barrier_semaphore()

    def greet(k, carry):
        pl.semaphore_signal(
            barrier, inc=1, device_id={"buf": rem(me + k, 32)}, device_id_type=MESH
        )
        return carry

    lax.fori_loop(1, 32, greet, 0)
    for k in (1, 2, 4, 6, 7):
        pl.semaphore_signal(barrier, inc=1, device_id={"lat": rem(owner + k, 8)}, device_id_type=MESH)

    buf_copy = pltpu.make_async_copy(buf_hbm, buf, own_sem)
    buf_copy.start()
    loads = [pltpu.make_async_copy(win_hbm.at[pl.ds(0, ONE), :], cen, in_sem.at[4])]
    for p in range(4):
        low = pl.multiple_of(ONE + rem(owner + 8 - p, 8) * SUB, 16)
        loads.append(pltpu.make_async_copy(
            win_hbm.at[pl.ds(low, SUB), :], cen_pair.at[pl.ds(p * SUB, SUB), :], in_sem.at[p]
        ))
    for load in loads:
        load.start()

    rows = rows_ref[...]
    offset = rows - me * 256
    mine = (offset >= 0) & (offset < 256)
    lanes = lax.broadcasted_iota(jnp.int32, (8, 128), 1)
    key = (lanes * 256 + offset).astype(jnp.float32)
    first, last = [], []
    for g in range(4):
        here = mine & (lanes >= g * 32) & (lanes < g * 32 + 32)
        first.append(jnp.min(jnp.where(here, key, 32767.0), axis=1, keepdims=True))
        last.append(jnp.max(jnp.where(here, key, 0.0), axis=1, keepdims=True))
    chosen = jnp.concatenate(first + last, axis=0).astype(jnp.int32)
    hot = jnp.bitwise_and(chosen, 255) == lax.broadcasted_iota(jnp.int32, (64, 256), 1)
    hot = hot.astype(jnp.float32).astype(jnp.bfloat16)
    buf_copy.wait()
    for q in range(8):
        piece = jnp.dot(
            hot, buf[:, q * 512:(q + 1) * 512], preferred_element_type=jnp.float32
        )
        for r in range(2):
            for g in range(4):
                stage[g, pl.ds(r * 8 + q, 32, stride=16), :] = (
                    piece[r * 32:r * 32 + 32, g * 128:(g + 1) * 128]
                )
    for g in range(4):
        send[:, g * 128:(g + 1) * 128] = stage[g].astype(jnp.bfloat16)

    pl.semaphore_wait(barrier, 36)

    def block_of(device):
        dc = rem(device, 2)
        dchip = device // 2
        dx, dy = dchip // 4, rem(dchip, 4)
        return dc * 16 + (dy + dc * (dx - dy)) * 4 + dx + dc * (dy - dx)

    def tile16(ref, index):
        return ref.at[pl.ds(pl.multiple_of(index * 16, 16), 16), :]

    def place(block):
        return rem(block, 4) * 8 + block // 4

    def push(k, carry):
        far = 32 - k
        tx, ty = rem(x + far // 8, 4), rem(y + rem(far, 8) // 2, 4)
        target = (tx * 4 + ty) * 2 + rem(core + far, 2)
        pltpu.make_async_remote_copy(
            src_ref=tile16(send, place(block_of(target))),
            dst_ref=tile16(recv, me),
            send_sem=a2a_send,
            recv_sem=a2a_recv,
            device_id={"buf": target},
            device_id_type=MESH,
        ).start()
        return carry

    lax.fori_loop(1, 32, push, 0)
    my_block = core * 16 + b * 4 + a
    own_copy = pltpu.make_async_copy(tile16(send, place(my_block)), tile16(recv, me), own_sem)
    own_copy.start()
    scale_copy = pltpu.make_async_remote_copy(
        src_ref=scale_ref, dst_ref=scale_pair, send_sem=z_send.at[0], recv_sem=z_recv.at[0],
        device_id={"lat": opposite}, device_id_type=MESH,
    )
    scale_copy.start()

    for load in loads:
        load.wait()

    def center(t, carry):
        at = pl.ds(pl.multiple_of(t * 32, 32), 32)
        cen[at, :] = (cen[at, :].astype(jnp.float32) - bias_ref[...]).astype(jnp.bfloat16)
        return carry

    def center_pair(t, carry):
        at = pl.ds(pl.multiple_of(t * 32, 32), 32)
        cen_pair[at, :] = (
            cen_pair[at, :].astype(jnp.float32) - bias_ref[...]
        ).astype(jnp.bfloat16)
        return carry

    lax.fori_loop(0, ONE // 32, center, 0)
    lax.fori_loop(0, 4 * SUB // 32, center_pair, 0)

    own_copy.wait()
    pltpu.make_async_copy(recv.at[pl.ds(0, 496), :], recv.at[pl.ds(0, 496), :], a2a_recv).wait()

    own = jnp.broadcast_to(rows_ref[pl.ds(my_block // 4, 1), :], (32, 128))
    own = lax.shift_right_logical(own, 8).astype(jnp.float32)
    entry = lax.broadcasted_iota(jnp.int32, (32, 128), 0)
    peer = lax.broadcasted_iota(jnp.int32, (32, 128), 1) - rem(my_block, 4) * 32
    source = jnp.sum(jnp.where(entry == peer, own, 0.0), axis=1, keepdims=True)
    twin = (own == source) & (peer >= 0) & (peer < entry)
    rank = jnp.sum(jnp.where(twin, 1.0, 0.0), axis=1, keepdims=True)
    code = (source * 16.0 + rank * 8.0).astype(jnp.int32)
    code = jnp.concatenate([code + q for q in range(8)], axis=0)
    hot = code == lax.broadcasted_iota(jnp.int32, (256, 512), 1)
    hot = hot.astype(jnp.float32).astype(jnp.bfloat16)
    picked[...] = jnp.dot(hot, recv[...], preferred_element_type=jnp.float32)
    squares = jnp.zeros((32, 512), jnp.float32)
    for q in range(8):
        value = picked[q * 32:q * 32 + 32, :]
        squares += value * value
    inverse = lax.rsqrt(jnp.sum(squares, axis=1, keepdims=True) + 1e-06)
    mine_at = pl.ds(pl.multiple_of(my_block * 32, 32), 32)
    for q in range(8):
        value = picked[q * 32:q * 32 + 32, :]
        units[0, mine_at, q * 512:q * 512 + 512] = (value * inverse).astype(jnp.bfloat16)

    def block_at(da, db):
        return core * 16 + rem(b + db + 4, 4) * 4 + rem(a + da + 4, 4)

    def device_at(da, db):
        pa, pb = rem(a + da + 4, 4), rem(b + db + 4, 4)
        px, py = pa + core * (pb - pa), pb + core * (pa - pb)
        return (px * 4 + py) * 2 + core

    sibling = me + 1 - 2 * core
    sent = [[], []]

    def block_ref(w, block, count=32, half=0):
        return units.at[w, pl.ds(pl.multiple_of(block * 32 + half * 16, 16), count), :]

    def give(w, block, target, count=32, half=0):
        at = block_ref(w, block, count, half)
        sem = ag_recv2 if half else ag_recv
        copy = pltpu.make_async_remote_copy(
            src_ref=at, dst_ref=at, send_sem=ag_send.at[w, len(sent[w])],
            recv_sem=sem.at[w, block], device_id={"buf": target}, device_id_type=MESH,
        )
        copy.start()
        sent[w].append(copy)

    def arrive(w, block, count=32, half=0):
        at = block_ref(w, block, count, half)
        sem = ag_recv2 if half else ag_recv
        pltpu.make_async_copy(at, at, sem.at[w, block]).wait()

    def spread(w, block):
        give(w, block, device_at(0, 1))
        give(w, block, device_at(0, -1))
        give(w, block, sibling)

    def second(w, da):
        block = block_at(da, -1)
        arrive(w, block)
        give(w, block, device_at(0, 1), 16, 0)
        give(w, block, sibling)
        block = block_at(da, 1)
        arrive(w, block)
        give(w, block, device_at(0, -1), 16, 1)
        give(w, block, sibling)

    def far(w, da):
        block = block_at(da, 2)
        arrive(w, block, 16, 0)
        arrive(w, block, 16, 1)
        give(w, block, sibling)

    def step(w, n):
        if n == 0:
            give(w, my_block, device_at(1, 0))
            give(w, my_block, device_at(-1, 0))
            spread(w, my_block)
        elif n == 1:
            block = block_at(-1, 0)
            arrive(w, block)
            give(w, block, device_at(1, 0), 16, 0)
            spread(w, block)
        elif n == 2:
            block = block_at(1, 0)
            arrive(w, block)
            give(w, block, device_at(-1, 0), 16, 1)
            spread(w, block)
        elif n == 3:
            second(w, 0)
        elif n == 4:
            block = block_at(2, 0)
            arrive(w, block, 16, 0)
            arrive(w, block, 16, 1)
            spread(w, block)
        elif n < 8:
            second(w, (-1, 1, 2)[n - 5])
        else:
            far(w, (0, -1, 1, 2)[n - 8])

    step(0, 0)
    z_copy = pltpu.make_async_remote_copy(
        src_ref=block_ref(0, my_block), dst_ref=block_ref(1, my_block),
        send_sem=z_send.at[1], recv_sem=z_recv.at[1],
        device_id={"lat": opposite}, device_id_type=MESH,
    )
    z_copy.start()
    for n in range(1, 8):
        step(0, n)

    def encode(group):
        at = pl.ds(pl.multiple_of(group * 256, 256), 256)
        scores = lax.dot_general(
            cen[...], units[0, at, :], NT, preferred_element_type=jnp.float32
        )
        act[:, at] = jnp.maximum(scores * scale_ref[:, at], 0.0).astype(jnp.bfloat16)

    def encode_pair(w, group):
        at = pl.ds(pl.multiple_of(group * 256, 256), 256)
        scale = (scale_pair if w else scale_ref)[:, at]
        scores = lax.dot_general(
            cen_pair[...], units[w, at, :], NT, preferred_element_type=jnp.float32
        )
        act_pair[w, :, at] = jnp.maximum(scores * scale, 0.0).astype(jnp.bfloat16)

    other = 1 - core
    other_b = x + core * (y - x)
    mine_near = core * 2 + b // 2
    mine_far = core * 2 + 1 - b // 2
    other_near = other * 2 + other_b // 2
    other_far = other * 2 + 1 - other_b // 2

    def arrive_group(w, group):
        def one(i, carry):
            arrive(w, group * 8 + i)
            return carry

        lax.fori_loop(0, 8, one, 0)

    encode(mine_near)
    arrive_group(0, other_near)
    encode(other_near)
    for n in range(8, 12):
        step(0, n)
    z_copy.wait_recv()
    step(1, 0)
    encode(mine_far)
    arrive_group(0, other_far)
    encode(other_far)

    def decode(target):
        columns = pl.ds(pl.multiple_of(target * 512, 512), 512)
        value = jnp.dot(act[...], units[0, :, columns], preferred_element_type=jnp.float32)
        part[target] = value.astype(jnp.bfloat16)

    def half_of(ref, half):
        return ref.at[pl.ds(half * HALF, HALF), :]

    def rs_copy(i, source, flow, way):
        return pltpu.make_async_remote_copy(
            src_ref=source, dst_ref=flow.at[i],
            send_sem=rs_send.at[way, i], recv_sem=rs_recv.at[way, i],
            device_id={"lat": left if way else right}, device_id_type=MESH,
        )

    def rs_wait(i, flow, way):
        pltpu.make_async_copy(flow.at[i], flow.at[i], rs_recv.at[way, i]).wait()

    def hop(i):
        for way, flow in ((0, flow_r), (1, flow_l)):
            low = ((i + way) % 2) * HALF
            away = 4 - (i + 1) // 2
            target = rem(owner + (8 - away if way else away), 8)
            rs_wait(i - 2, flow, way)
            total = flow[i - 2].astype(jnp.float32)
            total += part[target, low:low + HALF, :].astype(jnp.float32)
            flow[i - 2] = total.astype(jnp.bfloat16)
            rs_copy(i, flow.at[i - 2], flow, way).start()

    for way, flow in ((0, flow_r), (1, flow_l)):
        columns = pl.ds(pl.multiple_of(opposite * 512, 512), 512)
        rows_at = slice(way * HALF, way * HALF + HALF)
        value = jnp.dot(
            act[rows_at, :], units[0, :, columns], preferred_element_type=jnp.float32
        )
        part[opposite, rows_at, :] = value.astype(jnp.bfloat16)
        rs_copy(0, half_of(part.at[opposite], way), flow, way).start()

    def decode_next(i, carry):
        decode(rem(owner + 3 + 2 * i, 8))
        return carry

    lax.fori_loop(0, 2, decode_next, 0)
    rs_copy(1, half_of(part.at[rem(owner + 3, 8)], 1), flow_r, 0).start()
    rs_copy(1, half_of(part.at[rem(owner + 5, 8)], 0), flow_l, 1).start()
    step(1, 1)
    step(1, 2)

    def decode_rest(i, carry):
        decode(rem(owner + 6 + i, 8))
        return carry

    lax.fori_loop(0, 5, decode_rest, 0)
    step(1, 3)
    step(1, 4)
    hop(2)
    step(1, 5)
    lax.fori_loop(0, 4, lambda i, carry: (encode_pair(0, i), carry)[1], 0)
    hop(3)
    step(1, 6)
    scale_copy.wait_recv()
    hop(4)
    step(1, 7)
    encode_pair(1, mine_near)
    hop(5)
    for n in range(8, 12):
        step(1, n)
    arrive_group(1, other_near)
    encode_pair(1, other_near)
    encode_pair(1, mine_far)
    arrive_group(1, other_far)
    encode_pair(1, other_far)
    hop(6)

    def decode_pair(o, carry):
        columns = pl.ds(pl.multiple_of(rem(owner + o, 8) * 512, 512), 512)
        value = jnp.dot(act_pair[0], units[0, :, columns], preferred_element_type=jnp.float32)
        value += jnp.dot(act_pair[1], units[1, :, columns], preferred_element_type=jnp.float32)
        value = value.astype(jnp.bfloat16)
        for p in range(4):
            for c in range(PIECES):
                low = p * SUB + c * 16
                part_pair[c, p, o] = value[low:low + 16, :]
        return carry

    pair_copies = []

    def pair_give(way, c, p, source, dest, distance=1, slot=None):
        slot = p if slot is None else slot
        copy = pltpu.make_async_remote_copy(
            src_ref=source, dst_ref=dest,
            send_sem=pair_send.at[way, c, slot], recv_sem=pair_recv.at[way, c, slot],
            device_id={"lat": rem(owner + (8 - distance if way else distance), 8)},
            device_id_type=MESH,
        )
        copy.start()
        pair_copies.append(copy)

    def pair_wait(way, c, p):
        if p == 4:
            at = pair_far.at[way, c]
        else:
            at = pair_flow.at[way, c, p, pl.ds(0, 5 - p if p < 3 else 1)]
        pltpu.make_async_copy(at, at, pair_recv.at[way, c, p]).wait()

    lax.fori_loop(1, 8, decode_pair, 0)
    for c in range(PIECES):
        for way in range(2):
            source = part_pair.at[c, 3 if way else 0, pl.ds(3 if way else 1, 5)]
            pair_give(way, c, 0, source, pair_flow.at[way, c, 0])
    decode_pair(0, 0)

    bias = bias_ref[:, pl.ds(pl.multiple_of(owner * 512, 512), 512)]

    def out_copy(n):
        at = pl.ds(ONE, 768 - ONE) if n else pl.ds(0, ONE)
        return pltpu.make_async_copy(out_ref.at[at, :], out_hbm.at[at, :], in_sem.at[n])

    def finish_one():
        for i in (5, 6):
            rs_wait(i, flow_r, 0)
            rs_wait(i, flow_l, 1)
        for half in range(2):
            at = slice(half * HALF, half * HALF + HALF)
            total = part[owner, at, :].astype(jnp.float32) + bias
            total += flow_r[6 - half].astype(jnp.float32) + flow_l[5 + half].astype(jnp.float32)
            out_ref[at, :] = total.astype(jnp.bfloat16)
        out_copy(0).start()

    for p in range(1, 4):
        for c in range(PIECES):
            for way in range(2):
                pair_wait(way, c, p - 1)
                low = 0 if way else 1
                for k in range(5 - p):
                    mine_part = part_pair[c, 3 - p, 3 + p + k] if way else part_pair[c, p, 1 + k]
                    total = pair_flow[way, c, p - 1, low + k].astype(jnp.float32)
                    total += mine_part.astype(jnp.float32)
                    pair_flow[way, c, p - 1, low + k] = total.astype(jnp.bfloat16)
                source = pair_flow.at[way, c, p - 1, pl.ds(low, 5 - p)]
                if p < 3:
                    pair_give(way, c, p, source, pair_flow.at[way, c, p, pl.ds(0, 5 - p)])
                else:
                    pair_give(way, c, 4, source.at[0 if way else 1], pair_far.at[way, c], 2, 4)
                    pair_give(way, c, 3, source.at[1 if way else 0], pair_flow.at[way, c, 3, 0])
        if p == 1:
            finish_one()
    for c in range(PIECES):
        for way in range(2):
            pair_wait(way, c, 3)
            pair_wait(way, c, 4)

    for c in range(PIECES):
        for r in range(-4, 4):
            terms = []
            if -3 <= r <= 0:
                terms.append(part_pair[c, -r, 0])
            for p in range(4):
                if (r + 1 + p) % 8 == 0:
                    terms.append(pair_flow[0, c, p, 0])
                if (r + 2 - p) % 8 == 0:
                    terms.append(pair_flow[1, c, p, 4 - p if p < 3 else 0])
            if r == 3:
                terms.append(pair_far[0, c])
            if r == 2:
                terms.append(pair_far[1, c])
            total = jnp.broadcast_to(bias, (16, 512))
            for term in terms:
                total += term.astype(jnp.float32)
            low = pl.multiple_of(ONE + rem(owner + 8 + r, 8) * SUB + c * 16, 16)
            out_ref[pl.ds(low, 16), :] = total.astype(jnp.bfloat16)

    out_copy(1).start()

    pltpu.make_async_copy(send.at[pl.ds(0, 496), :], send.at[pl.ds(0, 496), :], a2a_send).wait()
    for copy in [scale_copy, z_copy] + sent[0] + sent[1] + pair_copies:
        copy.wait_send()

    def drain(i, carry):
        for way in range(2):
            pltpu.make_async_copy(flow_r.at[i], flow_r.at[i], rs_send.at[way, i]).wait()
        return carry

    lax.fori_loop(0, 7, drain, 0)
    out_copy(0).wait()
    out_copy(1).wait()


def on_device(buffer, sample_rows, window, enc_scale, dec_bias):
    vmem = pl.BlockSpec(memory_space=pltpu.VMEM)
    anywhere = pl.BlockSpec(memory_space=pl.ANY)
    call = pl.pallas_call(
        fused,
        out_shape=jax.ShapeDtypeStruct((768, 512), jnp.bfloat16),
        in_specs=[vmem, anywhere, anywhere, vmem, vmem],
        out_specs=anywhere,
        scratch_shapes=[
            pltpu.VMEM((768, 512), jnp.bfloat16),
            pltpu.VMEM((256, 4096), jnp.bfloat16),
            pltpu.VMEM((4, 512, 128), jnp.float32),
            pltpu.VMEM((512, 512), jnp.bfloat16),
            pltpu.VMEM((512, 512), jnp.bfloat16),
            pltpu.VMEM((256, 512), jnp.float32),
            pltpu.VMEM((2, 1024, 4096), jnp.bfloat16),
            pltpu.VMEM((ONE, 4096), jnp.bfloat16),
            pltpu.VMEM((4 * SUB, 4096), jnp.bfloat16),
            pltpu.VMEM((ONE, 1024), jnp.bfloat16),
            pltpu.VMEM((2, 4 * SUB, 1024), jnp.bfloat16),
            pltpu.VMEM((8, ONE, 512), jnp.bfloat16),
            pltpu.VMEM((7, HALF, 512), jnp.bfloat16),
            pltpu.VMEM((7, HALF, 512), jnp.bfloat16),
            pltpu.VMEM((PIECES, 4, 8, 16, 512), jnp.bfloat16),
            pltpu.VMEM((2, PIECES, 4, 5, 16, 512), jnp.bfloat16),
            pltpu.VMEM((2, PIECES, 16, 512), jnp.bfloat16),
            pltpu.VMEM((1, 1024), jnp.float32),
            pltpu.SemaphoreType.DMA((5,)),
            pltpu.SemaphoreType.DMA,
            pltpu.SemaphoreType.DMA,
            pltpu.SemaphoreType.DMA,
            pltpu.SemaphoreType.DMA((2,)),
            pltpu.SemaphoreType.DMA((2,)),
            pltpu.SemaphoreType.DMA((2, 40)),
            pltpu.SemaphoreType.DMA((2, 32)),
            pltpu.SemaphoreType.DMA((2, 32)),
            pltpu.SemaphoreType.DMA((2, 7)),
            pltpu.SemaphoreType.DMA((2, 7)),
            pltpu.SemaphoreType.DMA((2, PIECES, 5)),
            pltpu.SemaphoreType.DMA((2, PIECES, 5)),
        ],
        compiler_params=pltpu.CompilerParams(
            collective_id=0, has_side_effects=True, vmem_limit_bytes=52 * 1024 * 1024
        ),
    )
    return call(
        sample_rows.reshape(8, 128), buffer, window,
        enc_scale.reshape(1, 1024), dec_bias.reshape(1, 4096),
    )


def solution(mesh):
    in_specs = (P("buf", None), P("lat"), P("buf", None), P("lat"), P())
    out_specs = P("buf", "lat")
    return jax.shard_map(
        on_device, mesh=mesh, in_specs=in_specs, out_specs=out_specs, check_vma=False
    )
```
